512 devices in a mesh: dp: 64 (over x, y, core), mp: 8 (over z).
Axes of the slice: x: 4, y: 8, z: 8, core: 2. Of those that a mesh axis runs over, the one named last changes fastest.
Arguments:
- hidden: bfloat16 [98304, 3584], P('dp', 'mp'), may hold values from -6 to 6
- frozen_value_weight: bfloat16 [3584, 512], P('mp'), may hold values from -0.09375 to 0.09375
- adapter_down_weight: bfloat16 [64, 3584, 32], P('dp', 'mp'), may hold values from -0.09375 to 0.09375
- adapter_up_weight: bfloat16 [64, 32, 512], P('dp', None, 'mp'), may hold values from -1 to 1
- value_output_gradient: bfloat16 [98304, 512], P('dp', 'mp'), may hold values from -6 to 6
- sequence_tenant_index: int32 [128], P('dp'), may hold values from 0 to 63
- tenant_slot_table: int32 [64], replicated, may hold values from 0 to 63, each once
Outputs:
- values: bfloat16 [98304, 512], P('dp', 'mp')
- hidden_grad: bfloat16 [98304, 3584], P('dp', 'mp')
- down_grad: float32 [64, 3584, 32], P('dp', 'mp')
- up_grad: float32 [64, 32, 512], P('dp', None, 'mp')
The draws below stay inside these ranges and needn't reach their ends.
Inputs may be any that keep to these rules, and one draw needn't show every extreme that they name: `sequence_tenant_index`: tenant of each sequence; several sequences may share a tenant. `tenant_slot_table`: every slot holds exactly one tenant.
All inputs are finite; a program needn't handle non-finite values.
Results may differ from the reference program's by a relative error of at most 0.0039.
Values may be sent and summed in bfloat16 or wider, within the bound.
A program may use at most 128 MiB of HBM per device.

```python
import math
import jax
import jax.numpy as jnp
import numpy as np
from jax import lax

MODEL_WIDTH = 3584
VALUE_FEATURES = 512
ADAPTER_RANK = 32
LEN = 768
TENANT_SLOTS = 64
SEQS = 128
TOKENS = 98304


def set_ends(entries, own_key, smallest, largest):
    spot = [jax.random.randint(jax.random.fold_in(own_key, axis), (), 0, length) for axis, length in enumerate(entries.shape)]
    widest = entries.shape.index(max(entries.shape))
    beside = spot[:widest] + [(spot[widest] + 1) % entries.shape[widest]] + spot[widest + 1:]
    return entries.at[tuple(spot)].set(smallest).at[tuple(beside)].set(largest)


def shard_levels(own_key, extent, pieces, least, largest):
    gain = 1.0
    for axis_at, blocks in pieces:
        heights = jax.random.uniform(jax.random.fold_in(jax.random.fold_in(own_key, 6), axis_at), (blocks,), jnp.float32, least / len(pieces), largest / len(pieces))
        gain = gain * jnp.repeat(jnp.exp(heights), extent[axis_at] // blocks).reshape((-1,) + (1,) * (len(extent) - 1 - axis_at))
    return gain


def cumulative_ranks(count, skew):
    loads = [(1 << 20) // math.isqrt(rank ** skew) + 1 for rank in range(1, count + 1)]
    scale = 1 + sum(loads) // (1 << 30)
    return np.cumsum(np.array([max(1, weight // scale) for weight in loads]))


def skewed_ids(own_key, dims, amount, slope):
    listing = cumulative_ranks(amount, slope)
    ticket = jax.random.randint(jax.random.fold_in(own_key, 1), dims, 0, int(listing[amount - 1]))
    rank = jnp.searchsorted(jnp.asarray(listing, jnp.int32), ticket, side="right")
    return jax.random.permutation(jax.random.fold_in(own_key, 2), amount)[rank].astype(jnp.int32)


def scatter_about(own_key, extent, spread, most, cuts=(), kind=jnp.bfloat16):
    loudness = shard_levels(own_key, extent, cuts, -0.22, 0.18) if cuts else 1.0
    drawn = jax.random.normal(own_key, extent, jnp.float32) * spread * loudness
    return jnp.minimum(jnp.maximum(drawn, -most), most).astype(kind)


def setup_inputs(seed: int = 0) -> dict:
    seeds = jax.random.split(jax.random.key(seed), 8)
    return {
        "hidden": scatter_about(seeds[0], (TOKENS, MODEL_WIDTH), 1.0, 6.0, ((0, 64), (1, 8))),
        "frozen_value_weight": scatter_about(seeds[1], (MODEL_WIDTH, VALUE_FEATURES), MODEL_WIDTH ** -0.5, 0.09375, ((0, 8),)),
        "adapter_down_weight": scatter_about(seeds[2], (TENANT_SLOTS, MODEL_WIDTH, ADAPTER_RANK), MODEL_WIDTH ** -0.5, 0.09375, ((0, 64), (1, 8))),
        "adapter_up_weight": scatter_about(seeds[3], (TENANT_SLOTS, ADAPTER_RANK, VALUE_FEATURES), ADAPTER_RANK ** -0.5, 1.0, ((0, 64), (2, 8))),
        "value_output_gradient": scatter_about(seeds[4], (TOKENS, VALUE_FEATURES), 1.0, 6.0, ((0, 64), (1, 8))),
        "sequence_tenant_index": set_ends(skewed_ids(seeds[5], (SEQS,), TENANT_SLOTS, 2), jax.random.fold_in(seeds[5], 3), 0, TENANT_SLOTS - 1).astype(jnp.int32),
        "tenant_slot_table": jax.random.permutation(seeds[6], TENANT_SLOTS).astype(jnp.int32),
    }


highest_precision = lax.Precision.HIGHEST


def reference(hidden, frozen_value_weight, adapter_down_weight, adapter_up_weight, value_output_gradient, sequence_tenant_index, tenant_slot_table):
    slot_ids = tenant_slot_table[sequence_tenant_index].astype(jnp.int32)
    sequence_input_rows = hidden.reshape(SEQS, LEN, MODEL_WIDTH)
    seq_grads = value_output_gradient.reshape(SEQS, LEN, VALUE_FEATURES)

    def per_sequence(seq_items):
        x_seq, g_seq, adapter_slot_index = seq_items
        chosen_down_factor = adapter_down_weight[adapter_slot_index]
        chosen_up_factor = adapter_up_weight[adapter_slot_index]
        reduced_rank_partial = jnp.dot(x_seq, chosen_down_factor, preferred_element_type=jnp.float32)
        adapter_output_term = jnp.dot(reduced_rank_partial, chosen_up_factor.astype(jnp.float32), precision=highest_precision)
        frozen_value_output = jnp.dot(x_seq, frozen_value_weight, preferred_element_type=jnp.float32)
        projected_values = (frozen_value_output + adapter_output_term).astype(jnp.bfloat16)
        backward_lowrank_term = jnp.dot(g_seq, chosen_up_factor.T, preferred_element_type=jnp.float32).astype(jnp.bfloat16)
        grad_in = jnp.dot(g_seq, frozen_value_weight.T, preferred_element_type=jnp.float32)
        grad_in = grad_in + jnp.dot(backward_lowrank_term, chosen_down_factor.T, preferred_element_type=jnp.float32)
        down_term = jnp.dot(x_seq.T, backward_lowrank_term, preferred_element_type=jnp.float32)
        up_term = jnp.dot(reduced_rank_partial.T, g_seq.astype(jnp.float32), precision=highest_precision)
        return projected_values, grad_in.astype(jnp.bfloat16), down_term, up_term

    projected_values, grad_in, down_terms, up_terms = lax.map(per_sequence, (sequence_input_rows, seq_grads, slot_ids))
    down_grad = jax.ops.segment_sum(down_terms, slot_ids, num_segments=TENANT_SLOTS)
    up_grad = jax.ops.segment_sum(up_terms, slot_ids, num_segments=TENANT_SLOTS)
    return (projected_values.reshape(TOKENS, VALUE_FEATURES), grad_in.reshape(TOKENS, MODEL_WIDTH), down_grad, up_grad)
```

```python
import functools

import jax
import jax.numpy as jnp
from jax import lax
from jax.experimental import pallas as pl
from jax.experimental.pallas import tpu as pltpu
from jax.sharding import PartitionSpec as P

F32 = jnp.float32
BF16 = jnp.bfloat16
MESH = pl.DeviceIdType.MESH
NY = 8


def nt(a, b):
    return lax.dot_general(a, b, (((1,), (1,)), ((), ())), preferred_element_type=F32)


def nn(a, b):
    return jnp.dot(a, b, preferred_element_type=F32)


def iota(shape, dim):
    return lax.broadcasted_iota(jnp.int32, shape, dim)


def onehot(mask):
    return jnp.where(mask, 1.0, 0.0).astype(BF16)


def split(v):
    hi = v.astype(BF16)
    return hi, (v - hi.astype(F32)).astype(BF16)


def kernel(
    ny, nl, nz,
    idx_ref, tab_ref, g_hbm, b_hbm, a_hbm, w_hbm, x_hbm,
    values_ref, hgrad_hbm, down_ref, up_ref,
    b_in, w, wt, x, hg, bt,
    gbuf, pb, rs_send, rs_recv,
    ids, m1, col_a, line_a_out, line_a, col_b, line_b_out, line_b, z_b,
    u_out, u_in, line_d, col_d_out, col_d, line_u, col_u_out, col_u,
    ab, low, back_t, a_rows,
    in_sem, out_sem, ag_s, ag_r, rs_s, rs_r,
    ids_s, ids_r, ca_s, ca_r, la_s, la_r, cb_s, cb_r, lb_s, lb_r, zb_s, zb_r,
    zu_s, zu_r, ld_s, ld_r, cd_s, cd_r, lu_s, lu_r, cu_s, cu_r,
):
    rank, cols = b_in.shape
    width, tokens = x.shape
    features = w.shape[1]
    rows = tokens // 2
    half = cols // 2
    chunk = 256 if rows % 256 == 0 else rows
    d, z = lax.axis_index("dp"), lax.axis_index("mp")
    c = lax.rem(d, 2)
    y = lax.rem(lax.div(d, 2), ny)
    xx = lax.div(d, 2 * ny)
    line = xx * 2 + c

    def line_peer(o):
        other = lax.rem(line + o, nl)
        return ((lax.div(other, 2) * ny + y) * 2 + lax.rem(other, 2), z)

    def col_peer(o):
        return ((xx * ny + lax.rem(y + o, ny)) * 2 + c, z)

    def z_peer(o):
        return (d, lax.rem(z + o, nz))

    barrier = pltpu.get_barrier_semaphore()
    peers = [z_peer(o) for o in range(1, nz)]
    peers += [col_peer(o) for o in range(1, ny)]
    peers += [line_peer(o) for o in range(1, nl)]
    for peer in peers:
        pl.semaphore_signal(barrier, inc=1, device_id=peer, device_id_type=MESH)

    loads = []
    for i, (src, dst) in enumerate(
        ((g_hbm, gbuf.at[z]), (b_hbm, b_in), (a_hbm, col_a.at[pl.ds(0, rank), :]), (w_hbm, w), (x_hbm, x))
    ):
        copy = pltpu.make_async_copy(src, dst, in_sem.at[i])
        copy.start()
        loads.append(copy)

    pending = []

    def send(src, dst, send_sem, recv_sem, peer):
        copy = pltpu.make_async_remote_copy(
            src_ref=src, dst_ref=dst, send_sem=send_sem, recv_sem=recv_sem,
            device_id=peer, device_id_type=MESH,
        )
        copy.start()
        pending.append(copy)
        return copy

    def block(ref, o, size):
        return ref.at[pl.ds(o * size, size), :]

    def exchange(out, into, size, send_sem, recv_sem, peer, n, same=False):
        return [
            send(
                block(out, 0 if same else o, size), block(into, o, size),
                send_sem.at[o], recv_sem.at[o], peer(o),
            )
            for o in range(1, n)
        ]

    def arrive(copies):
        for copy in copies:
            copy.wait_recv()

    s0, s1 = tab_ref[idx_ref[0]], tab_ref[idx_ref[1]]
    row, lane = iota((8, 128), 0), iota((8, 128), 1)
    second = jnp.where(row == 2, lax.shift_right_logical(lane, 5) & 1, row & 1)
    ids[0:8, :] = jnp.where(second == 1, s1, s0)

    low_half = iota((1, 128), 1) < cols

    def swapped(v):
        return pltpu.roll(v, cols, 1)

    loads[1].wait()
    wide = onehot(iota((cols, 128), 0) == iota((cols, 128), 1))
    col_b[0:rank, :] = nn(b_in[...], wide).astype(BF16)
    loads[0].wait()
    loads[2].wait()
    pl.semaphore_wait(barrier, len(peers))

    most = nz // 2
    hops = ((most, most - 1), (most - 1, most))

    def toward(direction, n):
        return lax.rem(z + (n if direction == 0 else nz - n), nz)

    def ring_peer(direction):
        return (d, toward(direction, 1))

    ag = {}

    def ag_send(direction, h, t):
        part = gbuf.at[toward(1 - direction, t) if t else z, pl.ds(h * half, half), :]
        ag[direction, h, t] = send(
            part, part, ag_s.at[direction, h, t], ag_r.at[direction, h, t], ring_peer(direction)
        )

    served = set()

    def ag_serve(t):
        if t >= most or ("ag", t) in served:
            return
        served.add(("ag", t))
        for h in range(2):
            for direction in range(2):
                n = hops[direction][h]
                if t < n:
                    ag[direction, h, t].wait_recv()
                    if t + 1 < n:
                        ag_send(direction, h, t + 1)

    for h in range(2):
        for direction in range(2):
            if hops[direction][h]:
                ag_send(direction, h, 0)
    got_ids = exchange(ids, ids, 8, ids_s, ids_r, line_peer, nl, same=True)
    got_cb = exchange(col_b, col_b, rank, cb_s, cb_r, col_peer, ny, same=True)
    got_ca = exchange(col_a, col_a, rank, ca_s, ca_r, col_peer, ny, same=True)

    loads[3].wait()
    square = onehot(iota((features, features), 0) == iota((features, features), 1))
    wt[...] = nt(square, w[...]).astype(BF16)
    loads[4].wait()

    def base(step, carry):
        at = pl.ds(pl.multiple_of(step * chunk, chunk), chunk)
        part = nn(wt[...], x[:, at])
        for j in range(nz):
            pb[j, :, at] = part[j * cols : (j + 1) * cols, :]
        return carry

    lax.fori_loop(0, tokens // chunk, base, 0)

    arrive(got_ids)
    slot_in = (xx * ny + lax.rem(y + ny - lax.shift_right_logical(iota((rank, ny * rank), 1), 5), ny)) * 2 + c
    same_rank = (iota((rank, ny * rank), 1) & 31) == iota((rank, ny * rank), 0)
    for p in range(nl):
        q = (nl - p) % nl
        for s in range(2):
            own = ids[q * 8 + s : q * 8 + s + 1, :][:, 0:1]
            m1[(p * 2 + s) * rank : (p * 2 + s + 1) * rank, :] = onehot((slot_in == own) & same_rank)
    arrive(got_cb)
    line_b_out[...] = nn(m1[...], col_b[...]).astype(BF16)
    got_lb = exchange(line_b_out, line_b, 2 * rank, lb_s, lb_r, line_peer, nl)
    ag_serve(0)
    arrive(got_ca)
    line_a_out[...] = nn(m1[...], col_a[...]).astype(BF16)
    got_la = exchange(line_a_out, line_a, 2 * rank, la_s, la_r, line_peer, nl)

    def gathered(out, into, size, n):
        total = out[0:size, :].astype(F32)
        for o in range(1, n):
            total = total + into[o * size : (o + 1) * size, :].astype(F32)
        return total

    arrive(got_lb)
    mine = gathered(line_b_out, line_b, 2 * rank, nl)
    z_b[z] = (mine[0:rank, :] + swapped(mine[rank:, :])).astype(BF16)
    got_zb = [
        send(z_b.at[z], z_b.at[z], zb_s.at[o], zb_r.at[o], z_peer(o)) for o in range(1, nz)
    ]
    ag_serve(1)

    arrive(got_la)
    ab[...] = gathered(line_a_out, line_a, 2 * rank, nl).astype(BF16)
    for s in range(2):
        part = nn(ab[s * rank : (s + 1) * rank, :], x[:, s * rows : (s + 1) * rows])
        hi, rest = split(part)
        low[2 * s * rank : (2 * s + 1) * rank, :] = hi
        low[(2 * s + 1) * rank : (2 * s + 2) * rank, :] = rest
    ag_serve(2)
    arrive(got_zb)
    blocks = [z_b[j].astype(F32) for j in range(nz)]
    tiles = features // 128
    up = [
        [jnp.where(low_half, blocks[2 * i], swapped(blocks[2 * i + 1])) for i in range(tiles)],
        [jnp.where(low_half, swapped(blocks[2 * i]), blocks[2 * i + 1]) for i in range(tiles)],
    ]
    up = [jnp.concatenate(parts, axis=1).astype(BF16) for parts in up]
    for s in range(2):
        bt[s] = nt(square, jnp.concatenate([up[s], up[s]], axis=0)).astype(BF16)

        def adapt(step, carry):
            here = pl.ds(pl.multiple_of(step * chunk, chunk), chunk)
            at = pl.ds(pl.multiple_of(s * rows + step * chunk, chunk), chunk)
            part = nn(bt[s], low[2 * s * rank : 2 * (s + 1) * rank, here])
            for j in range(nz):
                pb[j, :, at] += part[j * cols : (j + 1) * cols, :]
            return carry

        lax.fori_loop(0, rows // chunk, adapt, 0)

    rs = {}

    def rs_go(direction, h, t):
        n = hops[direction][h]
        value = pb[toward(direction, n - t), h * half : (h + 1) * half, :]
        if t:
            value = value + rs_recv[direction, h, t - 1].astype(F32)
        rs_send[direction, h, t] = value.astype(BF16)
        rs[direction, h, t] = send(
            rs_send.at[direction, h, t], rs_recv.at[direction, h, t],
            rs_s.at[direction, h, t], rs_r.at[direction, h, t], ring_peer(direction),
        )

    def rs_serve(t):
        if t >= most or ("rs", t) in served:
            return
        served.add(("rs", t))
        for h in range(2):
            for direction in range(2):
                n = hops[direction][h]
                if t < n:
                    rs[direction, h, t].wait_recv()
                    if t + 1 < n:
                        rs_go(direction, h, t + 1)

    for h in range(2):
        for direction in range(2):
            if hops[direction][h]:
                rs_go(direction, h, 0)

    ag_serve(most - 1)

    def grads(s, at=None):
        at = pl.ds(s * rows, rows) if at is None else at
        return gbuf[:, :, at].reshape(nz * cols, at.size)

    ups = []
    for s in range(2):
        both = nt(low[2 * s * rank : 2 * (s + 1) * rank, :], grads(s))
        ups.append(both[0:rank, :] + both[rank:, :])
    for i in range(tiles):
        t0, t1 = (u[:, i * 128 : (i + 1) * 128] for u in ups)
        u_out[2 * i] = jnp.where(low_half, t0, swapped(t1)).astype(BF16)
        u_out[2 * i + 1] = jnp.where(low_half, swapped(t0), t1).astype(BF16)
    got_zu = [
        send(u_out.at[lax.rem(z + o, nz)], u_in.at[o], zu_s.at[o], zu_r.at[o], z_peer(o))
        for o in range(1, nz)
    ]
    for s in range(2):
        back_t[s * rank : (s + 1) * rank, :] = nn(up[s], grads(s)).astype(BF16)
        line_d[s * rank : (s + 1) * rank, :] = nt(
            back_t[s * rank : (s + 1) * rank, :], x[:, s * rows : (s + 1) * rows]
        ).astype(BF16)
    got_ld = exchange(line_d, line_d, 2 * rank, ld_s, ld_r, line_peer, nl, same=True)
    rs_serve(0)

    turn = onehot(iota((width, width), 0) == iota((width, width), 1))
    a_rows[...] = nt(turn, ab[...]).astype(BF16)

    def input_grad(s):
        def body(step, carry):
            here = pl.ds(pl.multiple_of(step * chunk, chunk), chunk)
            at = pl.ds(pl.multiple_of(s * rows + step * chunk, chunk), chunk)
            hg[:, at] = (
                nn(w[...], grads(s, at))
                + nn(a_rows[:, s * rank : (s + 1) * rank], back_t[s * rank : (s + 1) * rank, here])
            ).astype(BF16)
            return carry

        lax.fori_loop(0, rows // chunk, body, 0)
        at = pl.ds(s * rows, rows)
        copy = pltpu.make_async_copy(hg.at[:, at], hgrad_hbm.at[:, at], out_sem.at[s])
        copy.start()
        return copy

    stores = [input_grad(0)]
    arrive(got_zu)
    total = u_out[z].astype(F32)
    for o in range(1, nz):
        total = total + u_in[o].astype(F32)
    for s, part in enumerate((total, swapped(total))):
        line_u[s * rank : (s + 1) * rank, :] = jnp.where(low_half, part, 0.0).astype(BF16)
    got_lu = exchange(line_u, line_u, 2 * rank, lu_s, lu_r, line_peer, nl, same=True)
    rs_serve(1)

    arrive(got_ld)
    per_tile = 128 // (2 * rank)
    across = []
    for i in range(nl // per_tile):
        q = i * per_tile
        across.append(jnp.where(low_half, ids[q * 8 + 2 : q * 8 + 3, :], ids[q * 8 + 10 : q * 8 + 11, :]))
    across = jnp.concatenate(across, axis=1)
    shape = (ny * rank, nl * 2 * rank)
    slot_out = (xx * ny + lax.rem(y + lax.shift_right_logical(iota((ny * rank, 1), 0), 5), ny)) * 2 + c
    m2 = onehot((slot_out == across) & ((iota(shape, 1) & 31) == (iota(shape, 0) & 31)))
    summed = nn(m2, line_d[...])
    col_d_out[...] = summed.astype(BF16)
    got_cd = exchange(col_d_out, col_d, rank, cd_s, cd_r, col_peer, ny)
    own_d = summed[0:rank, :]
    arrive(got_lu)
    summed_u = nn(m2, line_u[...])
    col_u_out[...] = summed_u.astype(BF16)
    got_cu = exchange(col_u_out, col_u, rank, cu_s, cu_r, col_peer, ny)
    own_u = summed_u[0:rank, :]
    rs_serve(2)
    stores.append(input_grad(1))
    rs_serve(most - 1)
    for h in range(2):
        value = pb[z, h * half : (h + 1) * half, :]
        for direction in range(2):
            n = hops[direction][h]
            if n:
                value = value + rs_recv[direction, h, n - 1].astype(F32)
        values_ref[h * half : (h + 1) * half, :] = value.astype(BF16)

    arrive(got_cd)
    for o in range(1, ny):
        own_d = own_d + col_d[o * rank : (o + 1) * rank, :].astype(F32)
    down_ref[...] = own_d
    arrive(got_cu)
    for o in range(1, ny):
        own_u = own_u + col_u[o * rank : (o + 1) * rank, :].astype(F32)
    up_ref[...] = own_u[:, 0:cols]
    for copy in pending:
        copy.wait_send()
    for copy in stores:
        copy.wait()


def local(ny, nl, nz, hidden, weight, down, up, grad, index, table):
    tokens, width = hidden.shape
    rank = down.shape[2]
    cols = grad.shape[1]
    features = weight.shape[1]
    rows, half = tokens // 2, cols // 2
    most = nz // 2
    vm = pltpu.VMEM
    dma = pltpu.SemaphoreType.DMA
    scratch = [
        vm((rank, cols), BF16), vm((width, features), BF16), vm((features, width), BF16),
        vm((width, tokens), BF16), vm((width, tokens), BF16), vm((2, features, 2 * rank), BF16),
        vm((nz, cols, tokens), BF16), vm((nz, cols, tokens), F32),
        vm((2, 2, most, half, tokens), BF16), vm((2, 2, most, half, tokens), BF16),
        vm((8 * nl, 128), jnp.int32), vm((nl * 2 * rank, ny * rank), BF16),
        vm((ny * rank, width), BF16), vm((nl * 2 * rank, width), BF16), vm((nl * 2 * rank, width), BF16),
        vm((ny * rank, 128), BF16), vm((nl * 2 * rank, 128), BF16), vm((nl * 2 * rank, 128), BF16),
        vm((nz, rank, 128), BF16),
        vm((nz, rank, 128), BF16), vm((nz, rank, 128), BF16),
        vm((nl * 2 * rank, width), BF16), vm((ny * rank, width), BF16), vm((ny * rank, width), BF16),
        vm((nl * 2 * rank, 128), BF16), vm((ny * rank, 128), BF16), vm((ny * rank, 128), BF16),
        vm((2 * rank, width), BF16), vm((4 * rank, rows), BF16), vm((2 * rank, rows), BF16),
        vm((width, 2 * rank), BF16),
        dma((5,)), dma((2,)),
        dma((2, 2, most)), dma((2, 2, most)), dma((2, 2, most)), dma((2, 2, most)),
    ]
    for n in (nl, ny, nl, ny, nl, nz, nz, nl, ny, nl, ny):
        scratch += [dma((n,)), dma((n,))]
    anywhere = pl.BlockSpec(memory_space=pl.ANY)
    inside = pl.BlockSpec(memory_space=pltpu.VMEM)
    scalars = pl.BlockSpec(memory_space=pltpu.SMEM)
    values, hidden_grad, down_t, up_grad = pl.pallas_call(
        functools.partial(kernel, ny, nl, nz),
        out_shape=(
            jax.ShapeDtypeStruct((cols, tokens), BF16),
            jax.ShapeDtypeStruct((width, tokens), BF16),
            jax.ShapeDtypeStruct((rank, width), F32),
            jax.ShapeDtypeStruct((rank, cols), F32),
        ),
        in_specs=[scalars, scalars] + [anywhere] * 5,
        out_specs=(inside, anywhere, inside, inside),
        scratch_shapes=scratch,
        compiler_params=pltpu.CompilerParams(collective_id=0, has_side_effects=True),
        name="adapter_step",
    )(index, table, grad.T, up[0], down[0].T, weight, hidden.T)
    return values.T, hidden_grad.T, down_t.T[None], up_grad[None]


def build(mesh, ny):
    nl, nz = mesh.shape["dp"] // ny, mesh.shape["mp"]
    return jax.shard_map(
        functools.partial(local, ny, nl, nz),
        mesh=mesh,
        in_specs=(
            P("dp", "mp"),
            P("mp", None),
            P("dp", "mp", None),
            P("dp", None, "mp"),
            P("dp", "mp"),
            P("dp"),
            P(),
        ),
        out_specs=(P("dp", "mp"), P("dp", "mp"), P("dp", "mp", None), P("dp", None, "mp")),
        check_vma=False,
    )


def solution(mesh):
    return build(mesh, NY)
```

```python
import functools

import jax
import jax.numpy as jnp
from jax import lax
from jax.experimental import pallas as pl
from jax.experimental.pallas import tpu as pltpu
from jax.sharding import PartitionSpec as P

F32 = jnp.float32
BF16 = jnp.bfloat16
MESH = pl.DeviceIdType.MESH
NY = 8


def nt(a, b):
    return lax.dot_general(a, b, (((1,), (1,)), ((), ())), preferred_element_type=F32)


def nn(a, b):
    return jnp.dot(a, b, preferred_element_type=F32)


def iota(shape, dim):
    return lax.broadcasted_iota(jnp.int32, shape, dim)


def onehot(mask):
    return jnp.where(mask, 1.0, 0.0).astype(BF16)


def split(v):
    hi = v.astype(BF16)
    return hi, (v - hi.astype(F32)).astype(BF16)


def pieces(width):
    first = (width // 2 + 127) // 128 * 128
    return [(at, size) for at, size in ((0, first), (first, width - first)) if size]


def kernel(
    ny, nl, nz,
    idx_hbm, tab_hbm, g_hbm, b_hbm, a_hbm, w_hbm, x_hbm,
    values_ref, hgrad_hbm, down_ref, up_ref,
    idx_ref, tab_ref, b_in, w, wt, x, hg, bt,
    gbuf, pb, rs_send, rs_recv,
    ids, m1, m2, col_b, line_b_out, line_b, z_b, u_out, u_in, line_u, col_u_out, col_u,
    low, back_t, a_rows,
    in_sem, out_sem, ag_s, ag_r, rs_s, rs_r,
    ids_s, ids_r, cb_s, cb_r, lb_s, lb_r, zb_s, zb_r, zu_s, zu_r, lu_s, lu_r, cu_s, cu_r,
    *by_piece,
):
    rank, cols = b_in.shape
    width, tokens = x.shape
    features = w.shape[1]
    rows = tokens // 2
    half = cols // 2
    chunk = 256 if rows % 256 == 0 else rows
    cuts = pieces(width)
    parts = range(len(cuts))
    col_a, line_a_out, line_a, ab, line_d, col_d_out, col_d = (
        by_piece[i * len(cuts) : (i + 1) * len(cuts)] for i in range(7)
    )
    ca_s, ca_r, la_s, la_r, ld_s, ld_r, cd_s, cd_r = by_piece[7 * len(cuts) :]
    d, z = lax.axis_index("dp"), lax.axis_index("mp")
    c = lax.rem(d, 2)
    y = lax.rem(lax.div(d, 2), ny)
    xx = lax.div(d, 2 * ny)
    line = xx * 2 + c

    def line_peer(o):
        other = lax.rem(line + o, nl)
        return ((lax.div(other, 2) * ny + y) * 2 + lax.rem(other, 2), z)

    def col_peer(o):
        return ((xx * ny + lax.rem(y + o, ny)) * 2 + c, z)

    def z_peer(o):
        return (d, lax.rem(z + o, nz))

    barrier = pltpu.get_barrier_semaphore()
    peers = [z_peer(o) for o in range(1, nz)]
    peers += [col_peer(o) for o in range(1, ny)]
    peers += [line_peer(o) for o in range(1, nl)]
    for peer in peers:
        pl.semaphore_signal(barrier, inc=1, device_id=peer, device_id_type=MESH)

    loads = []
    wanted = [(idx_hbm, idx_ref), (tab_hbm, tab_ref), (g_hbm, gbuf.at[z]), (b_hbm, b_in)]
    wanted += [(a_hbm.at[:, pl.ds(*cuts[p])], col_a[p].at[pl.ds(0, rank), :]) for p in parts]
    wanted += [(w_hbm, w), (x_hbm, x)]
    for i, (src, dst) in enumerate(wanted):
        copy = pltpu.make_async_copy(src, dst, in_sem.at[i])
        copy.start()
        loads.append(copy)

    pending = []

    def send(src, dst, send_sem, recv_sem, peer):
        copy = pltpu.make_async_remote_copy(
            src_ref=src, dst_ref=dst, send_sem=send_sem, recv_sem=recv_sem,
            device_id=peer, device_id_type=MESH,
        )
        copy.start()
        pending.append(copy)
        return copy

    def block(ref, o, size):
        return ref.at[pl.ds(o * size, size), :]

    def exchange(out, into, size, send_sem, recv_sem, peer, n, same=False):
        return [
            send(
                block(out, 0 if same else o, size), block(into, o, size),
                send_sem.at[o], recv_sem.at[o], peer(o),
            )
            for o in range(1, n)
        ]

    def arrive(copies):
        for copy in copies:
            copy.wait_recv()

    loads[0].wait()
    loads[1].wait()
    s0, s1 = tab_ref[idx_ref[0]], tab_ref[idx_ref[1]]
    row, lane = iota((8, 128), 0), iota((8, 128), 1)
    second = jnp.where(row == 2, lax.shift_right_logical(lane, 5) & 1, row & 1)
    ids[0:8, :] = jnp.where(second == 1, s1, s0)

    low_half = iota((1, 128), 1) < cols

    def swapped(v):
        return pltpu.roll(v, cols, 1)

    loads[3].wait()
    wide = onehot(iota((cols, 128), 0) == iota((cols, 128), 1))
    col_b[0:rank, :] = nn(b_in[...], wide).astype(BF16)
    loads[2].wait()
    for p in parts:
        loads[4 + p].wait()
    pl.semaphore_wait(barrier, len(peers))

    most = nz // 2
    hops = ((most, most - 1), (most - 1, most))

    def toward(direction, n):
        return lax.rem(z + (n if direction == 0 else nz - n), nz)

    def ring_peer(direction):
        return (d, toward(direction, 1))

    ag = {}

    def ag_send(direction, h, t):
        part = gbuf.at[toward(1 - direction, t) if t else z, pl.ds(h * half, half), :]
        ag[direction, h, t] = send(
            part, part, ag_s.at[direction, h, t], ag_r.at[direction, h, t], ring_peer(direction)
        )

    served = set()

    def ag_serve(t, *halves):
        for h in halves:
            if ("ag", t, h) in served:
                continue
            served.add(("ag", t, h))
            for direction in range(2):
                n = hops[direction][h]
                if t < n:
                    ag[direction, h, t].wait_recv()
                    if t + 1 < n:
                        ag_send(direction, h, t + 1)

    for h in range(2):
        for direction in range(2):
            if hops[direction][h]:
                ag_send(direction, h, 0)
    got_ids = exchange(ids, ids, 8, ids_s, ids_r, line_peer, nl, same=True)
    got_cb = exchange(col_b, col_b, rank, cb_s, cb_r, col_peer, ny, same=True)
    got_ca = [
        exchange(col_a[p], col_a[p], rank, ca_s.at[p], ca_r.at[p], col_peer, ny, same=True) for p in parts
    ]

    loads[-2].wait()
    square = onehot(iota((features, features), 0) == iota((features, features), 1))
    wt[...] = nt(square, w[...]).astype(BF16)
    loads[-1].wait()

    def base(step, carry):
        at = pl.ds(pl.multiple_of(step * chunk, chunk), chunk)
        part = nn(wt[...], x[:, at])
        for j in range(nz):
            pb[j, :, at] = part[j * cols : (j + 1) * cols, :]
        return carry

    lax.fori_loop(0, tokens // chunk, base, 0)

    arrive(got_ids)
    slot_in = (xx * ny + lax.rem(y + ny - lax.shift_right_logical(iota((rank, ny * rank), 1), 5), ny)) * 2 + c
    same_rank = (iota((rank, ny * rank), 1) & 31) == iota((rank, ny * rank), 0)
    for p in range(nl):
        q = (nl - p) % nl
        for s in range(2):
            own = ids[q * 8 + s : q * 8 + s + 1, :][:, 0:1]
            m1[(p * 2 + s) * rank : (p * 2 + s + 1) * rank, :] = onehot((slot_in == own) & same_rank)
    def gathered(out, into, size, n):
        total = out[0:size, :].astype(F32)
        for o in range(1, n):
            total = total + into[o * size : (o + 1) * size, :].astype(F32)
        return total

    def pick_a(p):
        arrive(got_ca[p])
        line_a_out[p][...] = nn(m1[...], col_a[p][...]).astype(BF16)
        return exchange(line_a_out[p], line_a[p], 2 * rank, la_s.at[p], la_r.at[p], line_peer, nl)

    ag_serve(0, 0)
    arrive(got_cb)
    line_b_out[...] = nn(m1[...], col_b[...]).astype(BF16)
    got_lb = exchange(line_b_out, line_b, 2 * rank, lb_s, lb_r, line_peer, nl)
    got_la = [pick_a(0)]
    ag_serve(0, 1)
    arrive(got_lb)
    mine = gathered(line_b_out, line_b, 2 * rank, nl)
    z_b[z] = (mine[0:rank, :] + swapped(mine[rank:, :])).astype(BF16)
    got_zb = [
        send(z_b.at[z], z_b.at[z], zb_s.at[o], zb_r.at[o], z_peer(o)) for o in range(1, nz)
    ]
    ag_serve(1, 0)
    got_la += [pick_a(p) for p in parts[1:]]
    ag_serve(1, 1)
    ag_serve(2, 0)
    arrive(got_zb)
    blocks = [z_b[j].astype(F32) for j in range(nz)]
    tiles = features // 128
    up = [
        [jnp.where(low_half, blocks[2 * i], swapped(blocks[2 * i + 1])) for i in range(tiles)],
        [jnp.where(low_half, swapped(blocks[2 * i]), blocks[2 * i + 1]) for i in range(tiles)],
    ]
    up = [jnp.concatenate(parts, axis=1).astype(BF16) for parts in up]
    for s in range(2):
        bt[s] = nt(square, jnp.concatenate([up[s], up[s]], axis=0)).astype(BF16)

    ag_serve(2, 1)
    for p in parts:
        arrive(got_la[p])
        ab[p][...] = gathered(line_a_out[p], line_a[p], 2 * rank, nl).astype(BF16)
    for s in range(2):
        part = 0.0
        for p in parts:
            at, size = cuts[p]
            part = part + nn(ab[p][s * rank : (s + 1) * rank, :], x[at : at + size, s * rows : (s + 1) * rows])
        hi, rest = split(part)
        low[2 * s * rank : (2 * s + 1) * rank, :] = hi
        low[(2 * s + 1) * rank : (2 * s + 2) * rank, :] = rest

    for s in range(2):

        def adapt(step, carry):
            here = pl.ds(pl.multiple_of(step * chunk, chunk), chunk)
            at = pl.ds(pl.multiple_of(s * rows + step * chunk, chunk), chunk)
            part = nn(bt[s], low[2 * s * rank : 2 * (s + 1) * rank, here])
            for j in range(nz):
                pb[j, :, at] += part[j * cols : (j + 1) * cols, :]
            return carry

        lax.fori_loop(0, rows // chunk, adapt, 0)

    rs = {}

    def rs_go(direction, h, t):
        n = hops[direction][h]
        value = pb[toward(direction, n - t), h * half : (h + 1) * half, :]
        if t:
            value = value + rs_recv[direction, h, t - 1].astype(F32)
        rs_send[direction, h, t] = value.astype(BF16)
        rs[direction, h, t] = send(
            rs_send.at[direction, h, t], rs_recv.at[direction, h, t],
            rs_s.at[direction, h, t], rs_r.at[direction, h, t], ring_peer(direction),
        )

    def rs_serve(t, *halves):
        for h in halves:
            if ("rs", t, h) in served:
                continue
            served.add(("rs", t, h))
            for direction in range(2):
                n = hops[direction][h]
                if t < n:
                    rs[direction, h, t].wait_recv()
                    if t + 1 < n:
                        rs_go(direction, h, t + 1)

    for h in range(2):
        for direction in range(2):
            if hops[direction][h]:
                rs_go(direction, h, 0)

    for t in range(most):
        ag_serve(t, 0, 1)

    def grads(s, at=None):
        at = pl.ds(s * rows, rows) if at is None else at
        return gbuf[:, :, at].reshape(nz * cols, at.size)

    got_ld = []
    for s in range(2):
        back_t[s * rank : (s + 1) * rank, :] = nn(up[s], grads(s)).astype(BF16)
    for p in parts:
        at, size = cuts[p]
        for s in range(2):
            line_d[p][s * rank : (s + 1) * rank, :] = nt(
                back_t[s * rank : (s + 1) * rank, :], x[at : at + size, s * rows : (s + 1) * rows]
            ).astype(BF16)
        got_ld.append(
            exchange(line_d[p], line_d[p], 2 * rank, ld_s.at[p], ld_r.at[p], line_peer, nl, same=True)
        )
    ups = []
    for s in range(2):
        both = nt(low[2 * s * rank : 2 * (s + 1) * rank, :], grads(s))
        ups.append(both[0:rank, :] + both[rank:, :])
    for i in range(tiles):
        t0, t1 = (u[:, i * 128 : (i + 1) * 128] for u in ups)
        u_out[2 * i] = jnp.where(low_half, t0, swapped(t1)).astype(BF16)
        u_out[2 * i + 1] = jnp.where(low_half, swapped(t0), t1).astype(BF16)
    got_zu = [
        send(u_out.at[lax.rem(z + o, nz)], u_in.at[o], zu_s.at[o], zu_r.at[o], z_peer(o))
        for o in range(1, nz)
    ]
    per_tile = 128 // (2 * rank)
    across = []
    for i in range(nl // per_tile):
        q = i * per_tile
        across.append(jnp.where(low_half, ids[q * 8 + 2 : q * 8 + 3, :], ids[q * 8 + 10 : q * 8 + 11, :]))
    across = jnp.concatenate(across, axis=1)
    shape = (ny * rank, nl * 2 * rank)
    slot_out = (xx * ny + lax.rem(y + lax.shift_right_logical(iota((ny * rank, 1), 0), 5), ny)) * 2 + c
    m2[...] = onehot((slot_out == across) & ((iota(shape, 1) & 31) == (iota(shape, 0) & 31)))
    for p in parts:
        at, size = cuts[p]
        turn = onehot(iota((size, size), 0) == iota((size, size), 1))
        a_rows[at : at + size, :] = nt(turn, ab[p][...]).astype(BF16)

    def input_grad(s):
        def body(step, carry):
            here = pl.ds(pl.multiple_of(step * chunk, chunk), chunk)
            at = pl.ds(pl.multiple_of(s * rows + step * chunk, chunk), chunk)
            hg[:, at] = (
                nn(w[...], grads(s, at))
                + nn(a_rows[:, s * rank : (s + 1) * rank], back_t[s * rank : (s + 1) * rank, here])
            ).astype(BF16)
            return carry

        lax.fori_loop(0, rows // chunk, body, 0)
        at = pl.ds(s * rows, rows)
        copy = pltpu.make_async_copy(hg.at[:, at], hgrad_hbm.at[:, at], out_sem.at[s])
        copy.start()
        return copy

    rs_serve(0, 0)
    stores = [input_grad(0)]
    rs_serve(0, 1)
    got_cd, own_d = [], []

    def spread_d(p):
        arrive(got_ld[p])
        summed = nn(m2[...], line_d[p][...])
        col_d_out[p][...] = summed.astype(BF16)
        got_cd.append(
            exchange(col_d_out[p], col_d[p], rank, cd_s.at[p], cd_r.at[p], col_peer, ny)
        )
        own_d.append(summed[0:rank, :])

    spread_d(0)
    arrive(got_zu)
    total = u_out[z].astype(F32)
    for o in range(1, nz):
        total = total + u_in[o].astype(F32)
    for s, part in enumerate((total, swapped(total))):
        line_u[s * rank : (s + 1) * rank, :] = jnp.where(low_half, part, 0.0).astype(BF16)
    got_lu = exchange(line_u, line_u, 2 * rank, lu_s, lu_r, line_peer, nl, same=True)
    rs_serve(1, 0)
    for p in parts[1:]:
        spread_d(p)
    rs_serve(1, 1)
    arrive(got_lu)
    summed_u = nn(m2[...], line_u[...])
    col_u_out[...] = summed_u.astype(BF16)
    got_cu = exchange(col_u_out, col_u, rank, cu_s, cu_r, col_peer, ny)
    own_u = summed_u[0:rank, :]
    stores.append(input_grad(1))
    for t in range(2, most):
        rs_serve(t, 0)
        rs_serve(t, 1)
    for h in range(2):
        value = pb[z, h * half : (h + 1) * half, :]
        for direction in range(2):
            n = hops[direction][h]
            if n:
                value = value + rs_recv[direction, h, n - 1].astype(F32)
        values_ref[h * half : (h + 1) * half, :] = value.astype(BF16)

    for p in parts:
        arrive(got_cd[p])
        for o in range(1, ny):
            own_d[p] = own_d[p] + col_d[p][o * rank : (o + 1) * rank, :].astype(F32)
        down_ref[:, cuts[p][0] : cuts[p][0] + cuts[p][1]] = own_d[p]
    arrive(got_cu)
    for o in range(1, ny):
        own_u = own_u + col_u[o * rank : (o + 1) * rank, :].astype(F32)
    up_ref[...] = own_u[:, 0:cols]
    for copy in pending:
        copy.wait_send()
    for copy in stores:
        copy.wait()


def place_results(*refs):
    sources, results, held, sems = refs[:4], refs[4:8], refs[8:12], refs[12]
    jobs = []
    for source, result, via in zip(sources, results, held):
        size = source.shape[0] // (4 if source.shape[0] % 64 == 0 else 1)
        jobs += [
            tuple(ref.at[pl.ds(at, size), :] for ref in (source, via, result))
            for at in range(0, source.shape[0], size)
        ]
    into = [pltpu.make_async_copy(s, v, sems.at[0, i]) for i, (s, v, _) in enumerate(jobs)]
    out = [pltpu.make_async_copy(v, r, sems.at[1, i]) for i, (_, v, r) in enumerate(jobs)]
    for copy in into:
        copy.start()
    for first, second in zip(into, out):
        first.wait()
        second.start()
    for copy in out:
        copy.wait()


def local(ny, nl, nz, hidden, weight, down, up, grad, index, table):
    tokens, width = hidden.shape
    rank = down.shape[2]
    cols = grad.shape[1]
    features = weight.shape[1]
    rows, half = tokens // 2, cols // 2
    most = nz // 2
    vm = pltpu.VMEM
    dma = pltpu.SemaphoreType.DMA
    cuts = pieces(width)
    scratch = [
        pltpu.SMEM(index.shape, jnp.int32), pltpu.SMEM(table.shape, jnp.int32),
        vm((rank, cols), BF16), vm((width, features), BF16), vm((features, width), BF16),
        vm((width, tokens), BF16), vm((width, tokens), BF16), vm((2, features, 2 * rank), BF16),
        vm((nz, cols, tokens), BF16), vm((nz, cols, tokens), F32),
        vm((2, 2, most, half, tokens), BF16), vm((2, 2, most, half, tokens), BF16),
        vm((8 * nl, 128), jnp.int32),
        vm((nl * 2 * rank, ny * rank), BF16), vm((ny * rank, nl * 2 * rank), BF16),
        vm((ny * rank, 128), BF16), vm((nl * 2 * rank, 128), BF16), vm((nl * 2 * rank, 128), BF16),
        vm((nz, rank, 128), BF16), vm((nz, rank, 128), BF16), vm((nz, rank, 128), BF16),
        vm((nl * 2 * rank, 128), BF16), vm((ny * rank, 128), BF16), vm((ny * rank, 128), BF16),
        vm((4 * rank, rows), BF16), vm((2 * rank, rows), BF16), vm((width, 2 * rank), BF16),
        dma((6 + len(cuts),)), dma((2,)),
        dma((2, 2, most)), dma((2, 2, most)), dma((2, 2, most)), dma((2, 2, most)),
    ]
    for n in (nl, ny, nl, nz, nz, nl, ny):
        scratch += [dma((n,)), dma((n,))]
    for n in (ny, 2 * nl, 2 * nl, 2, 2 * nl, ny, ny):
        scratch += [vm((n * rank, size), BF16) for _, size in cuts]
    for n in (ny, nl, nl, ny):
        scratch += [dma((len(cuts), n)), dma((len(cuts), n))]
    anywhere = pl.BlockSpec(memory_space=pl.ANY)
    inside = pl.BlockSpec(memory_space=pltpu.VMEM)
    values, hidden_grad, down_t, up_grad = pl.pallas_call(
        functools.partial(kernel, ny, nl, nz),
        out_shape=(
            jax.ShapeDtypeStruct((cols, tokens), BF16),
            jax.ShapeDtypeStruct((width, tokens), BF16),
            jax.ShapeDtypeStruct((rank, width), F32),
            jax.ShapeDtypeStruct((rank, cols), F32),
        ),
        in_specs=[pl.BlockSpec(memory_space=pltpu.HBM)] * 7,
        out_specs=(inside, anywhere, inside, inside),
        scratch_shapes=scratch,
        compiler_params=pltpu.CompilerParams(collective_id=0, has_side_effects=True),
        name="adapter_step",
    )(index, table, grad.T, up[0], down[0].T, weight, hidden.T)
    results = (values, hidden_grad, down_t, up_grad)
    values, hidden_grad, down_t, up_grad = pl.pallas_call(
        place_results,
        out_shape=tuple(jax.ShapeDtypeStruct(r.shape, r.dtype) for r in results),
        in_specs=[anywhere] * 4,
        out_specs=(pl.BlockSpec(memory_space=pltpu.HBM),) * 4,
        scratch_shapes=[vm(r.shape, r.dtype) for r in results] + [dma((2, 16))],
        name="place_results",
    )(*results)
    return values.T, hidden_grad.T, down_t.T[None], up_grad[None]


def build(mesh, ny):
    nl, nz = mesh.shape["dp"] // ny, mesh.shape["mp"]
    return jax.shard_map(
        functools.partial(local, ny, nl, nz),
        mesh=mesh,
        in_specs=(
            P("dp", "mp"),
            P("mp", None),
            P("dp", "mp", None),
            P("dp", None, "mp"),
            P("dp", "mp"),
            P("dp"),
            P(),
        ),
        out_specs=(P("dp", "mp"), P("dp", "mp"), P("dp", "mp", None), P("dp", None, "mp")),
        check_vma=False,
    )


def solution(mesh):
    return build(mesh, NY)
```

```python
import functools

import jax
import jax.numpy as jnp
from jax import lax
from jax.experimental import pallas as pl
from jax.experimental.pallas import tpu as pltpu
from jax.sharding import PartitionSpec as P

F32 = jnp.float32
BF16 = jnp.bfloat16
MESH = pl.DeviceIdType.MESH
QUARTERS = 4
NY = 8


def nt(a, b):
    return lax.dot_general(a, b, (((1,), (1,)), ((), ())), preferred_element_type=F32)


def nn(a, b):
    return jnp.dot(a, b, preferred_element_type=F32)


def iota(shape, dim):
    return lax.broadcasted_iota(jnp.int32, shape, dim)


def onehot(mask):
    return jnp.where(mask, 1.0, 0.0).astype(BF16)


def split(v):
    hi = v.astype(BF16)
    return hi, (v - hi.astype(F32)).astype(BF16)


def pieces(width):
    first = (width // 2 + 127) // 128 * 128
    return [(at, size) for at, size in ((0, first), (first, width - first)) if size]


def kernel(
    ny, nl, nz,
    idx_hbm, tab_hbm, g_hbm, b_hbm, a_hbm, w_hbm, x_hbm,
    values_ref, hgrad_hbm, down_ref, up_ref,
    idx_ref, tab_ref, b_in, w, wt, x, hg, bt,
    gbuf, pb, rs_send, rs_recv,
    ids, m1, m2, col_b, line_b_out, line_b, z_b, u_out, u_in, line_u, col_u_out, col_u,
    low, back_t, a_rows,
    in_sem, out_sem, ag_s, ag_r, rs_s, rs_r,
    ids_s, ids_r, cb_s, cb_r, lb_s, lb_r, zb_s, zb_r, zu_s, zu_r, lu_s, lu_r, cu_s, cu_r,
    *by_piece,
):
    rank, cols = b_in.shape
    width, tokens = x.shape
    features = w.shape[1]
    rows = tokens // 2
    part_rows = cols // QUARTERS
    chunk = 256 if rows % 256 == 0 else rows
    cuts = pieces(width)
    parts = range(len(cuts))
    col_a, line_a_out, line_a, ab, line_d, col_d_out, col_d = (
        by_piece[i * len(cuts) : (i + 1) * len(cuts)] for i in range(7)
    )
    ca_s, ca_r, la_s, la_r, ld_s, ld_r, cd_s, cd_r = by_piece[7 * len(cuts) :]
    d, z = lax.axis_index("dp"), lax.axis_index("mp")
    c = lax.rem(d, 2)
    y = lax.rem(lax.div(d, 2), ny)
    xx = lax.div(d, 2 * ny)
    line = xx * 2 + c

    def line_peer(o):
        other = lax.rem(line + o, nl)
        return ((lax.div(other, 2) * ny + y) * 2 + lax.rem(other, 2), z)

    def col_peer(o):
        return ((xx * ny + lax.rem(y + o, ny)) * 2 + c, z)

    def z_peer(o):
        return (d, lax.rem(z + o, nz))

    barrier = pltpu.get_barrier_semaphore()
    peers = [z_peer(o) for o in range(1, nz)]
    peers += [col_peer(o) for o in range(1, ny)]
    peers += [line_peer(o) for o in range(1, nl)]
    for peer in peers:
        pl.semaphore_signal(barrier, inc=1, device_id=peer, device_id_type=MESH)

    loads = []
    wanted = [(idx_hbm, idx_ref), (tab_hbm, tab_ref), (g_hbm, gbuf.at[z]), (b_hbm, b_in)]
    wanted += [(a_hbm.at[:, pl.ds(*cuts[p])], col_a[p].at[pl.ds(0, rank), :]) for p in parts]
    wanted += [(w_hbm, w), (x_hbm, x)]
    for i, (src, dst) in enumerate(wanted):
        copy = pltpu.make_async_copy(src, dst, in_sem.at[i])
        copy.start()
        loads.append(copy)

    pending = []

    def send(src, dst, send_sem, recv_sem, peer):
        copy = pltpu.make_async_remote_copy(
            src_ref=src, dst_ref=dst, send_sem=send_sem, recv_sem=recv_sem,
            device_id=peer, device_id_type=MESH,
        )
        copy.start()
        pending.append(copy)
        return copy

    def block(ref, o, size):
        return ref.at[pl.ds(o * size, size), :]

    def exchange(out, into, size, send_sem, recv_sem, peer, n, same=False):
        return [
            send(
                block(out, 0 if same else o, size), block(into, o, size),
                send_sem.at[o], recv_sem.at[o], peer(o),
            )
            for o in range(1, n)
        ]

    def arrive(copies):
        for copy in copies:
            copy.wait_recv()

    loads[0].wait()
    loads[1].wait()
    s0, s1 = tab_ref[idx_ref[0]], tab_ref[idx_ref[1]]
    row, lane = iota((8, 128), 0), iota((8, 128), 1)
    second = jnp.where(row == 2, lax.shift_right_logical(lane, 5) & 1, row & 1)
    ids[0:8, :] = jnp.where(second == 1, s1, s0)

    low_half = iota((1, 128), 1) < cols

    def swapped(v):
        return pltpu.roll(v, cols, 1)

    loads[3].wait()
    wide = onehot(iota((cols, 128), 0) == iota((cols, 128), 1))
    col_b[0:rank, :] = nn(b_in[...], wide).astype(BF16)
    loads[2].wait()
    for p in parts:
        loads[4 + p].wait()
    pl.semaphore_wait(barrier, len(peers))

    most = nz // 2
    hops = [[most - ((h < QUARTERS // 2) == bool(side)) for h in range(QUARTERS)] for side in range(2)]

    def toward(direction, n):
        return lax.rem(z + (n if direction == 0 else nz - n), nz)

    def ring_peer(direction):
        return (d, toward(direction, 1))

    ag = {}

    def ag_send(direction, h, t):
        part = gbuf.at[toward(1 - direction, t) if t else z, pl.ds(h * part_rows, part_rows), :]
        ag[direction, h, t] = send(
            part, part, ag_s.at[direction, h, t], ag_r.at[direction, h, t], ring_peer(direction)
        )

    served = set()

    def ag_serve(t, *sides):
        for h in [h for h in range(QUARTERS) if h * 2 // QUARTERS in sides]:
            if ("ag", t, h) in served:
                continue
            served.add(("ag", t, h))
            for direction in range(2):
                n = hops[direction][h]
                if t < n:
                    ag[direction, h, t].wait_recv()
                    if t + 1 < n:
                        ag_send(direction, h, t + 1)

    for h in range(QUARTERS):
        for direction in range(2):
            if hops[direction][h]:
                ag_send(direction, h, 0)
    got_ids = exchange(ids, ids, 8, ids_s, ids_r, line_peer, nl, same=True)
    got_cb = exchange(col_b, col_b, rank, cb_s, cb_r, col_peer, ny, same=True)
    got_ca = [
        exchange(col_a[p], col_a[p], rank, ca_s.at[p], ca_r.at[p], col_peer, ny, same=True) for p in parts
    ]

    loads[-2].wait()
    square = onehot(iota((features, features), 0) == iota((features, features), 1))
    wt[...] = nt(square, w[...]).astype(BF16)
    loads[-1].wait()

    def base(step, carry):
        at = pl.ds(pl.multiple_of(step * chunk, chunk), chunk)
        part = nn(wt[...], x[:, at])
        for j in range(nz):
            pb[j, :, at] = part[j * cols : (j + 1) * cols, :]
        return carry

    lax.fori_loop(0, tokens // chunk, base, 0)

    arrive(got_ids)
    slot_in = (xx * ny + lax.rem(y + ny - lax.shift_right_logical(iota((rank, ny * rank), 1), 5), ny)) * 2 + c
    same_rank = (iota((rank, ny * rank), 1) & 31) == iota((rank, ny * rank), 0)
    for p in range(nl):
        q = (nl - p) % nl
        for s in range(2):
            own = ids[q * 8 + s : q * 8 + s + 1, :][:, 0:1]
            m1[(p * 2 + s) * rank : (p * 2 + s + 1) * rank, :] = onehot((slot_in == own) & same_rank)
    def gathered(out, into, size, n):
        total = out[0:size, :].astype(F32)
        for o in range(1, n):
            total = total + into[o * size : (o + 1) * size, :].astype(F32)
        return total

    def pick_a(p):
        arrive(got_ca[p])
        line_a_out[p][...] = nn(m1[...], col_a[p][...]).astype(BF16)
        return exchange(line_a_out[p], line_a[p], 2 * rank, la_s.at[p], la_r.at[p], line_peer, nl)

    ag_serve(0, 0)
    arrive(got_cb)
    line_b_out[...] = nn(m1[...], col_b[...]).astype(BF16)
    got_lb = exchange(line_b_out, line_b, 2 * rank, lb_s, lb_r, line_peer, nl)
    got_la = [pick_a(0)]
    ag_serve(0, 1)
    arrive(got_lb)
    mine = gathered(line_b_out, line_b, 2 * rank, nl)
    z_b[z] = (mine[0:rank, :] + swapped(mine[rank:, :])).astype(BF16)
    got_zb = [
        send(z_b.at[z], z_b.at[z], zb_s.at[o], zb_r.at[o], z_peer(o)) for o in range(1, nz)
    ]
    ag_serve(1, 0)
    got_la += [pick_a(p) for p in parts[1:]]
    ag_serve(1, 1)
    ag_serve(2, 0)
    for p in parts:
        arrive(got_la[p])
        ab[p][...] = gathered(line_a_out[p], line_a[p], 2 * rank, nl).astype(BF16)
    for s in range(2):
        part = 0.0
        for p in parts:
            at, size = cuts[p]
            part = part + nn(ab[p][s * rank : (s + 1) * rank, :], x[at : at + size, s * rows : (s + 1) * rows])
        hi, rest = split(part)
        low[2 * s * rank : (2 * s + 1) * rank, :] = hi
        low[(2 * s + 1) * rank : (2 * s + 2) * rank, :] = rest

    ag_serve(2, 1)
    arrive(got_zb)
    blocks = [z_b[j].astype(F32) for j in range(nz)]
    tiles = features // 128
    up = [
        [jnp.where(low_half, blocks[2 * i], swapped(blocks[2 * i + 1])) for i in range(tiles)],
        [jnp.where(low_half, swapped(blocks[2 * i]), blocks[2 * i + 1]) for i in range(tiles)],
    ]
    up = [jnp.concatenate(parts, axis=1).astype(BF16) for parts in up]
    for s in range(2):
        turned = nt(square, jnp.concatenate([up[s], up[s]], axis=0)).astype(BF16)
        bt[s] = turned.reshape(nz, cols, 2 * rank)

    def contribution(j, h):
        at = slice(h * part_rows, (h + 1) * part_rows)
        adapted = [
            nn(bt[s, j, at, :], low[2 * s * rank : 2 * (s + 1) * rank, :]) for s in range(2)
        ]
        return pb[j, at, :] + jnp.concatenate(adapted, axis=1)

    rs = {}

    def rs_go(direction, h, t):
        n = hops[direction][h]
        value = contribution(toward(direction, n - t), h)
        if t:
            value = value + rs_recv[direction, h, t - 1].astype(F32)
        rs_send[direction, h, t] = value.astype(BF16)
        rs[direction, h, t] = send(
            rs_send.at[direction, h, t], rs_recv.at[direction, h, t],
            rs_s.at[direction, h, t], rs_r.at[direction, h, t], ring_peer(direction),
        )

    def rs_serve(t, *sides):
        for h in [h for h in range(QUARTERS) if h * 2 // QUARTERS in sides]:
            if ("rs", t, h) in served:
                continue
            served.add(("rs", t, h))
            for direction in range(2):
                n = hops[direction][h]
                if t < n:
                    rs[direction, h, t].wait_recv()
                    if t + 1 < n:
                        rs_go(direction, h, t + 1)

    for h in range(QUARTERS):
        for direction in range(2):
            if hops[direction][h]:
                rs_go(direction, h, 0)

    for t in range(most):
        ag_serve(t, 0, 1)

    def grads(s, at=None):
        at = pl.ds(s * rows, rows) if at is None else at
        return gbuf[:, :, at].reshape(nz * cols, at.size)

    got_ld = []
    for s in range(2):
        back_t[s * rank : (s + 1) * rank, :] = nn(up[s], grads(s)).astype(BF16)
    for p in parts:
        at, size = cuts[p]
        for s in range(2):
            line_d[p][s * rank : (s + 1) * rank, :] = nt(
                back_t[s * rank : (s + 1) * rank, :], x[at : at + size, s * rows : (s + 1) * rows]
            ).astype(BF16)
        got_ld.append(
            exchange(line_d[p], line_d[p], 2 * rank, ld_s.at[p], ld_r.at[p], line_peer, nl, same=True)
        )
    ups = []
    for s in range(2):
        both = nt(low[2 * s * rank : 2 * (s + 1) * rank, :], grads(s))
        ups.append(both[0:rank, :] + both[rank:, :])
    for i in range(tiles):
        t0, t1 = (u[:, i * 128 : (i + 1) * 128] for u in ups)
        u_out[2 * i] = jnp.where(low_half, t0, swapped(t1)).astype(BF16)
        u_out[2 * i + 1] = jnp.where(low_half, swapped(t0), t1).astype(BF16)
    got_zu = [
        send(u_out.at[lax.rem(z + o, nz)], u_in.at[o], zu_s.at[o], zu_r.at[o], z_peer(o))
        for o in range(1, nz)
    ]
    per_tile = 128 // (2 * rank)
    across = []
    for i in range(nl // per_tile):
        q = i * per_tile
        across.append(jnp.where(low_half, ids[q * 8 + 2 : q * 8 + 3, :], ids[q * 8 + 10 : q * 8 + 11, :]))
    across = jnp.concatenate(across, axis=1)
    shape = (ny * rank, nl * 2 * rank)
    slot_out = (xx * ny + lax.rem(y + lax.shift_right_logical(iota((ny * rank, 1), 0), 5), ny)) * 2 + c
    m2[...] = onehot((slot_out == across) & ((iota(shape, 1) & 31) == (iota(shape, 0) & 31)))
    for p in parts:
        at, size = cuts[p]
        turn = onehot(iota((size, size), 0) == iota((size, size), 1))
        a_rows[at : at + size, :] = nt(turn, ab[p][...]).astype(BF16)

    def input_grad(s):
        def body(step, carry):
            here = pl.ds(pl.multiple_of(step * chunk, chunk), chunk)
            at = pl.ds(pl.multiple_of(s * rows + step * chunk, chunk), chunk)
            hg[:, at] = (
                nn(w[...], grads(s, at))
                + nn(a_rows[:, s * rank : (s + 1) * rank], back_t[s * rank : (s + 1) * rank, here])
            ).astype(BF16)
            return carry

        lax.fori_loop(0, rows // chunk, body, 0)
        at = pl.ds(s * rows, rows)
        copy = pltpu.make_async_copy(hg.at[:, at], hgrad_hbm.at[:, at], out_sem.at[s])
        copy.start()
        return copy

    rs_serve(0, 0)
    stores = [input_grad(0)]
    rs_serve(0, 1)
    got_cd, own_d = [], []

    def spread_d(p):
        arrive(got_ld[p])
        summed = nn(m2[...], line_d[p][...])
        col_d_out[p][...] = summed.astype(BF16)
        got_cd.append(
            exchange(col_d_out[p], col_d[p], rank, cd_s.at[p], cd_r.at[p], col_peer, ny)
        )
        own_d.append(summed[0:rank, :])

    spread_d(0)
    arrive(got_zu)
    total = u_out[z].astype(F32)
    for o in range(1, nz):
        total = total + u_in[o].astype(F32)
    for s, part in enumerate((total, swapped(total))):
        line_u[s * rank : (s + 1) * rank, :] = jnp.where(low_half, part, 0.0).astype(BF16)
    got_lu = exchange(line_u, line_u, 2 * rank, lu_s, lu_r, line_peer, nl, same=True)
    rs_serve(1, 0)
    for p in parts[1:]:
        spread_d(p)
    rs_serve(1, 1)
    arrive(got_lu)
    summed_u = nn(m2[...], line_u[...])
    col_u_out[...] = summed_u.astype(BF16)
    got_cu = exchange(col_u_out, col_u, rank, cu_s, cu_r, col_peer, ny)
    own_u = summed_u[0:rank, :]
    stores.append(input_grad(1))
    for t in range(2, most):
        rs_serve(t, 0)
        rs_serve(t, 1)
    for h in range(QUARTERS):
        value = contribution(z, h)
        for direction in range(2):
            n = hops[direction][h]
            if n:
                value = value + rs_recv[direction, h, n - 1].astype(F32)
        values_ref[h * part_rows : (h + 1) * part_rows, :] = value.astype(BF16)

    for p in parts:
        arrive(got_cd[p])
        for o in range(1, ny):
            own_d[p] = own_d[p] + col_d[p][o * rank : (o + 1) * rank, :].astype(F32)
        down_ref[:, cuts[p][0] : cuts[p][0] + cuts[p][1]] = own_d[p]
    arrive(got_cu)
    for o in range(1, ny):
        own_u = own_u + col_u[o * rank : (o + 1) * rank, :].astype(F32)
    up_ref[...] = own_u[:, 0:cols]
    for copy in pending:
        copy.wait_send()
    for copy in stores:
        copy.wait()


def place_results(*refs):
    sem = refs[8]
    copies = [pltpu.make_async_copy(refs[i], refs[4 + i], sem.at[i]) for i in range(4)]
    for copy in copies:
        copy.start()
    for copy in copies:
        copy.wait()


def local(ny, nl, nz, hidden, weight, down, up, grad, index, table):
    tokens, width = hidden.shape
    rank = down.shape[2]
    cols = grad.shape[1]
    features = weight.shape[1]
    rows, part_rows = tokens // 2, cols // QUARTERS
    most = nz // 2
    vm = pltpu.VMEM
    dma = pltpu.SemaphoreType.DMA
    cuts = pieces(width)
    scratch = [
        pltpu.SMEM(index.shape, jnp.int32), pltpu.SMEM(table.shape, jnp.int32),
        vm((rank, cols), BF16), vm((width, features), BF16), vm((features, width), BF16),
        vm((width, tokens), BF16), vm((width, tokens), BF16), vm((2, nz, cols, 2 * rank), BF16),
        vm((nz, cols, tokens), BF16), vm((nz, cols, tokens), F32),
        vm((2, QUARTERS, most, part_rows, tokens), BF16), vm((2, QUARTERS, most, part_rows, tokens), BF16),
        vm((8 * nl, 128), jnp.int32),
        vm((nl * 2 * rank, ny * rank), BF16), vm((ny * rank, nl * 2 * rank), BF16),
        vm((ny * rank, 128), BF16), vm((nl * 2 * rank, 128), BF16), vm((nl * 2 * rank, 128), BF16),
        vm((nz, rank, 128), BF16), vm((nz, rank, 128), BF16), vm((nz, rank, 128), BF16),
        vm((nl * 2 * rank, 128), BF16), vm((ny * rank, 128), BF16), vm((ny * rank, 128), BF16),
        vm((4 * rank, rows), BF16), vm((2 * rank, rows), BF16), vm((width, 2 * rank), BF16),
        dma((6 + len(cuts),)), dma((2,)),
        *([dma((2, QUARTERS, most))] * 4),
    ]
    for n in (nl, ny, nl, nz, nz, nl, ny):
        scratch += [dma((n,)), dma((n,))]
    for n in (ny, 2 * nl, 2 * nl, 2, 2 * nl, ny, ny):
        scratch += [vm((n * rank, size), BF16) for _, size in cuts]
    for n in (ny, nl, nl, ny):
        scratch += [dma((len(cuts), n)), dma((len(cuts), n))]
    anywhere = pl.BlockSpec(memory_space=pl.ANY)
    inside = pl.BlockSpec(memory_space=pltpu.VMEM)
    values, hidden_grad, down_t, up_grad = pl.pallas_call(
        functools.partial(kernel, ny, nl, nz),
        out_shape=(
            vm((cols, tokens), BF16), vm((width, tokens), BF16), vm((rank, width), F32), vm((rank, cols), F32)
        ),
        in_specs=[pl.BlockSpec(memory_space=pltpu.HBM)] * 7,
        out_specs=(inside, anywhere, inside, inside),
        scratch_shapes=scratch,
        compiler_params=pltpu.CompilerParams(collective_id=0, has_side_effects=True, vmem_limit_bytes=58 << 20),
        name="adapter_step",
    )(index, table, grad.T, up[0], down[0].T, weight, hidden.T)
    results = (values, hidden_grad, down_t, up_grad)
    values, hidden_grad, down_t, up_grad = pl.pallas_call(
        place_results,
        out_shape=tuple(jax.ShapeDtypeStruct(r.shape, r.dtype) for r in results),
        in_specs=[anywhere] * 4,
        out_specs=(pl.BlockSpec(memory_space=pltpu.HBM),) * 4,
        scratch_shapes=[dma((4,))],
        compiler_params=pltpu.CompilerParams(vmem_limit_bytes=4 << 20),
        name="place_results",
    )(*results)
    return values.T, hidden_grad.T, down_t.T[None], up_grad[None]


def build(mesh, ny):
    nl, nz = mesh.shape["dp"] // ny, mesh.shape["mp"]
    return jax.shard_map(
        functools.partial(local, ny, nl, nz),
        mesh=mesh,
        in_specs=(
            P("dp", "mp"),
            P("mp", None),
            P("dp", "mp", None),
            P("dp", None, "mp"),
            P("dp", "mp"),
            P("dp"),
            P(),
        ),
        out_specs=(P("dp", "mp"), P("dp", "mp"), P("dp", "mp", None), P("dp", None, "mp")),
        check_vma=False,
    )


def solution(mesh):
    return build(mesh, NY)
```

```python
import functools

import jax
import jax.numpy as jnp
from jax import lax
from jax.experimental import pallas as pl
from jax.experimental.pallas import tpu as pltpu
from jax.sharding import PartitionSpec as P

F32 = jnp.float32
BF16 = jnp.bfloat16
MESH = pl.DeviceIdType.MESH
QUARTERS = 4
NY = 8


def nt(a, b):
    return lax.dot_general(a, b, (((1,), (1,)), ((), ())), preferred_element_type=F32)


def nn(a, b):
    return jnp.dot(a, b, preferred_element_type=F32)


def iota(shape, dim):
    return lax.broadcasted_iota(jnp.int32, shape, dim)


def onehot(mask):
    return jnp.where(mask, 1.0, 0.0).astype(BF16)


def split(v):
    hi = v.astype(BF16)
    return hi, (v - hi.astype(F32)).astype(BF16)


def far_first(n):
    return sorted(range(1, n), key=lambda o: -min(o, n - o))


def pieces(width):
    first = (width // 2 + 127) // 128 * 128
    return [(at, size) for at, size in ((0, first), (first, width - first)) if size]


def kernel(
    ny, nl, nz,
    idx_hbm, tab_hbm, g_hbm, b_hbm, a_hbm, w_hbm, x_hbm,
    values_ref, hgrad_hbm, down_ref, up_ref,
    idx_ref, tab_ref, b_in, w, wt, x, hg, bt,
    gbuf, pb, rs_send, rs_recv,
    ids, m1, m2, col_b, line_b_out, line_b, z_b, u_out, u_in, line_u, col_u_out, col_u,
    low, back_t, a_rows,
    in_sem, out_sem, ag_s, ag_r, rs_s, rs_r,
    ids_s, ids_r, cb_s, cb_r, lb_s, lb_r, zb_s, zb_r, zu_s, zu_r, lu_s, lu_r, cu_s, cu_r,
    *by_piece,
):
    rank, cols = b_in.shape
    width, tokens = x.shape
    features = w.shape[1]
    rows = tokens // 2
    part_rows = cols // QUARTERS
    chunk = 256 if rows % 256 == 0 else rows
    cuts = pieces(width)
    parts = range(len(cuts))
    col_a, line_a_out, line_a, ab, line_d, col_d_out, col_d = (
        by_piece[i * len(cuts) : (i + 1) * len(cuts)] for i in range(7)
    )
    ca_s, ca_r, la_s, la_r, ld_s, ld_r, cd_s, cd_r = by_piece[7 * len(cuts) :]
    d, z = lax.axis_index("dp"), lax.axis_index("mp")
    c = lax.rem(d, 2)
    y = lax.rem(lax.div(d, 2), ny)
    xx = lax.div(d, 2 * ny)
    line = xx * 2 + c

    def line_peer(o):
        other = lax.rem(line + o, nl)
        return ((lax.div(other, 2) * ny + y) * 2 + lax.rem(other, 2), z)

    def col_peer(o):
        return ((xx * ny + lax.rem(y + o, ny)) * 2 + c, z)

    def z_peer(o):
        return (d, lax.rem(z + o, nz))

    barrier = pltpu.get_barrier_semaphore()
    peers = [z_peer(o) for o in range(1, nz)]
    peers += [col_peer(o) for o in range(1, ny)]
    peers += [line_peer(o) for o in range(1, nl)]
    for peer in peers:
        pl.semaphore_signal(barrier, inc=1, device_id=peer, device_id_type=MESH)

    loads = []
    wanted = [(idx_hbm, idx_ref), (tab_hbm, tab_ref), (g_hbm, gbuf.at[z]), (b_hbm, b_in)]
    wanted += [(a_hbm.at[:, pl.ds(*cuts[p])], col_a[p].at[pl.ds(0, rank), :]) for p in parts]
    wanted += [(w_hbm, w), (x_hbm, x)]
    for i, (src, dst) in enumerate(wanted):
        copy = pltpu.make_async_copy(src, dst, in_sem.at[i])
        copy.start()
        loads.append(copy)

    pending = []

    def send(src, dst, send_sem, recv_sem, peer):
        copy = pltpu.make_async_remote_copy(
            src_ref=src, dst_ref=dst, send_sem=send_sem, recv_sem=recv_sem,
            device_id=peer, device_id_type=MESH,
        )
        copy.start()
        pending.append(copy)
        return copy

    def block(ref, o, size):
        return ref.at[pl.ds(o * size, size), :]

    def exchange(out, into, size, send_sem, recv_sem, peer, n, same=False):
        return [
            send(
                block(out, 0 if same else o, size), block(into, o, size),
                send_sem.at[o], recv_sem.at[o], peer(o),
            )
            for o in far_first(n)
        ]

    def arrive(copies):
        for copy in copies:
            copy.wait_recv()

    loads[0].wait()
    loads[1].wait()
    s0, s1 = tab_ref[idx_ref[0]], tab_ref[idx_ref[1]]
    row, lane = iota((8, 128), 0), iota((8, 128), 1)
    second = jnp.where(row == 2, lax.shift_right_logical(lane, 5) & 1, row & 1)
    ids[0:8, :] = jnp.where(second == 1, s1, s0)

    low_half = iota((1, 128), 1) < cols

    def swapped(v):
        return pltpu.roll(v, cols, 1)

    loads[3].wait()
    wide = onehot(iota((cols, 128), 0) == iota((cols, 128), 1))
    col_b[0:rank, :] = nn(b_in[...], wide).astype(BF16)
    loads[2].wait()
    for p in parts:
        loads[4 + p].wait()
    pl.semaphore_wait(barrier, len(peers))

    most = nz // 2
    hops = [[most - ((h < QUARTERS // 2) == bool(side)) for h in range(QUARTERS)] for side in range(2)]

    def toward(direction, n):
        return lax.rem(z + (n if direction == 0 else nz - n), nz)

    def ring_peer(direction):
        return (d, toward(direction, 1))

    ag = {}

    def ag_send(direction, h, t):
        part = gbuf.at[toward(1 - direction, t) if t else z, pl.ds(h * part_rows, part_rows), :]
        ag[direction, h, t] = send(
            part, part, ag_s.at[direction, h, t], ag_r.at[direction, h, t], ring_peer(direction)
        )

    served = set()

    def ag_serve(t, *sides):
        for h in [h for h in range(QUARTERS) if h * 2 // QUARTERS in sides]:
            if ("ag", t, h) in served:
                continue
            served.add(("ag", t, h))
            for direction in range(2):
                n = hops[direction][h]
                if t < n:
                    ag[direction, h, t].wait_recv()
                    if t + 1 < n:
                        ag_send(direction, h, t + 1)

    for h in range(QUARTERS):
        for direction in range(2):
            if hops[direction][h]:
                ag_send(direction, h, 0)
    got_ids = exchange(ids, ids, 8, ids_s, ids_r, line_peer, nl, same=True)
    got_cb = exchange(col_b, col_b, rank, cb_s, cb_r, col_peer, ny, same=True)
    got_ca = [
        exchange(col_a[p], col_a[p], rank, ca_s.at[p], ca_r.at[p], col_peer, ny, same=True) for p in parts
    ]

    loads[-2].wait()
    square = onehot(iota((features, features), 0) == iota((features, features), 1))
    wt[...] = nt(square, w[...]).astype(BF16)
    loads[-1].wait()

    def base(step, carry):
        at = pl.ds(pl.multiple_of(step * chunk, chunk), chunk)
        part = nn(wt[...], x[:, at])
        for j in range(nz):
            pb[j, :, at] = part[j * cols : (j + 1) * cols, :]
        return carry

    lax.fori_loop(0, tokens // chunk, base, 0)

    arrive(got_ids)
    slot_in = (xx * ny + lax.rem(y + ny - lax.shift_right_logical(iota((rank, ny * rank), 1), 5), ny)) * 2 + c
    same_rank = (iota((rank, ny * rank), 1) & 31) == iota((rank, ny * rank), 0)
    for p in range(nl):
        q = (nl - p) % nl
        for s in range(2):
            own = ids[q * 8 + s : q * 8 + s + 1, :][:, 0:1]
            m1[(p * 2 + s) * rank : (p * 2 + s + 1) * rank, :] = onehot((slot_in == own) & same_rank)
    def gathered(out, into, size, n):
        total = out[0:size, :].astype(F32)
        for o in range(1, n):
            total = total + into[o * size : (o + 1) * size, :].astype(F32)
        return total

    def pick_a(p):
        arrive(got_ca[p])
        line_a_out[p][...] = nn(m1[...], col_a[p][...]).astype(BF16)
        return exchange(line_a_out[p], line_a[p], 2 * rank, la_s.at[p], la_r.at[p], line_peer, nl)

    ag_serve(0, 0)
    arrive(got_cb)
    line_b_out[...] = nn(m1[...], col_b[...]).astype(BF16)
    got_lb = exchange(line_b_out, line_b, 2 * rank, lb_s, lb_r, line_peer, nl)
    got_la = [pick_a(0)]
    ag_serve(0, 1)
    per_tile = 128 // (2 * rank)
    across = []
    for i in range(nl // per_tile):
        q = i * per_tile
        across.append(jnp.where(low_half, ids[q * 8 + 2 : q * 8 + 3, :], ids[q * 8 + 10 : q * 8 + 11, :]))
    across = jnp.concatenate(across, axis=1)
    shape = (ny * rank, nl * 2 * rank)
    slot_out = (xx * ny + lax.rem(y + lax.shift_right_logical(iota((ny * rank, 1), 0), 5), ny)) * 2 + c
    m2[...] = onehot((slot_out == across) & ((iota(shape, 1) & 31) == (iota(shape, 0) & 31)))
    arrive(got_lb)
    mine = gathered(line_b_out, line_b, 2 * rank, nl)
    z_b[z] = (mine[0:rank, :] + swapped(mine[rank:, :])).astype(BF16)
    got_zb = [
        send(z_b.at[z], z_b.at[z], zb_s.at[o], zb_r.at[o], z_peer(o)) for o in far_first(nz)
    ]
    ag_serve(1, 0)
    got_la += [pick_a(p) for p in parts[1:]]
    ag_serve(1, 1)
    ag_serve(2, 0)
    for p in parts:
        arrive(got_la[p])
        ab[p][...] = gathered(line_a_out[p], line_a[p], 2 * rank, nl).astype(BF16)
    for s in range(2):
        part = 0.0
        for p in parts:
            at, size = cuts[p]
            part = part + nn(ab[p][s * rank : (s + 1) * rank, :], x[at : at + size, s * rows : (s + 1) * rows])
        hi, rest = split(part)
        low[2 * s * rank : (2 * s + 1) * rank, :] = hi
        low[(2 * s + 1) * rank : (2 * s + 2) * rank, :] = rest

    for p in parts:
        at, size = cuts[p]
        turn = onehot(iota((size, size), 0) == iota((size, size), 1))
        a_rows[at : at + size, :] = nt(turn, ab[p][...]).astype(BF16)
    ag_serve(2, 1)
    arrive(got_zb)
    blocks = [z_b[j].astype(F32) for j in range(nz)]
    tiles = features // 128
    up = [
        [jnp.where(low_half, blocks[2 * i], swapped(blocks[2 * i + 1])) for i in range(tiles)],
        [jnp.where(low_half, swapped(blocks[2 * i]), blocks[2 * i + 1]) for i in range(tiles)],
    ]
    up = [jnp.concatenate(parts, axis=1).astype(BF16) for parts in up]
    for s in range(2):
        turned = nt(square, jnp.concatenate([up[s], up[s]], axis=0)).astype(BF16)
        bt[s] = turned.reshape(nz, cols, 2 * rank)

    def contribution(j, h):
        at = slice(h * part_rows, (h + 1) * part_rows)
        adapted = [
            nn(bt[s, j, at, :], low[2 * s * rank : 2 * (s + 1) * rank, :]) for s in range(2)
        ]
        return pb[j, at, :] + jnp.concatenate(adapted, axis=1)

    rs = {}

    def rs_go(direction, h, t):
        n = hops[direction][h]
        j = toward(direction, n - t)
        if t:
            value = pb[j, h * part_rows : (h + 1) * part_rows, :] + rs_recv[direction, h, t - 1].astype(F32)
        else:
            value = contribution(j, h)
        rs_send[direction, h, t] = value.astype(BF16)
        rs[direction, h, t] = send(
            rs_send.at[direction, h, t], rs_recv.at[direction, h, t],
            rs_s.at[direction, h, t], rs_r.at[direction, h, t], ring_peer(direction),
        )

    def rs_serve(t, *sides):
        for h in [h for h in range(QUARTERS) if h * 2 // QUARTERS in sides]:
            if ("rs", t, h) in served:
                continue
            served.add(("rs", t, h))
            for direction in range(2):
                n = hops[direction][h]
                if t < n:
                    rs[direction, h, t].wait_recv()
                    if t + 1 < n:
                        rs_go(direction, h, t + 1)

    def rs_begin(side):
        for h in [h for h in range(QUARTERS) if h * 2 // QUARTERS == side]:
            for direction in range(2):
                if hops[direction][h]:
                    rs_go(direction, h, 0)

    rs_begin(0)

    for t in range(most):
        ag_serve(t, 0, 1)

    def grads(s, at=None):
        at = pl.ds(s * rows, rows) if at is None else at
        return gbuf[:, :, at].reshape(nz * cols, at.size)

    got_ld = []
    for s in range(2):
        back_t[s * rank : (s + 1) * rank, :] = nn(up[s], grads(s)).astype(BF16)
    for p in parts:
        at, size = cuts[p]
        for s in range(2):
            line_d[p][s * rank : (s + 1) * rank, :] = nt(
                back_t[s * rank : (s + 1) * rank, :], x[at : at + size, s * rows : (s + 1) * rows]
            ).astype(BF16)
        got_ld.append(
            exchange(line_d[p], line_d[p], 2 * rank, ld_s.at[p], ld_r.at[p], line_peer, nl, same=True)
        )
    ups = []
    for s in range(2):
        both = nt(low[2 * s * rank : 2 * (s + 1) * rank, :], grads(s))
        ups.append(both[0:rank, :] + both[rank:, :])
    for i in range(tiles):
        t0, t1 = (u[:, i * 128 : (i + 1) * 128] for u in ups)
        u_out[2 * i] = jnp.where(low_half, t0, swapped(t1)).astype(BF16)
        u_out[2 * i + 1] = jnp.where(low_half, swapped(t0), t1).astype(BF16)
    got_zu = [
        send(u_out.at[lax.rem(z + o, nz)], u_in.at[o], zu_s.at[o], zu_r.at[o], z_peer(o))
        for o in far_first(nz)
    ]
    def input_grad(s):
        def body(step, carry):
            here = pl.ds(pl.multiple_of(step * chunk, chunk), chunk)
            at = pl.ds(pl.multiple_of(s * rows + step * chunk, chunk), chunk)
            hg[:, at] = (
                nn(w[...], grads(s, at))
                + nn(a_rows[:, s * rank : (s + 1) * rank], back_t[s * rank : (s + 1) * rank, here])
            ).astype(BF16)
            return carry

        lax.fori_loop(0, rows // chunk, body, 0)
        at = pl.ds(s * rows, rows)
        copy = pltpu.make_async_copy(hg.at[:, at], hgrad_hbm.at[:, at], out_sem.at[s])
        copy.start()
        return copy

    rs_begin(1)

    for s in range(2):
        turned = bt[s].reshape(nz * cols, 2 * rank)

        def adapt(step, carry):
            here = pl.ds(pl.multiple_of(step * chunk, chunk), chunk)
            at = pl.ds(pl.multiple_of(s * rows + step * chunk, chunk), chunk)
            part = nn(turned, low[2 * s * rank : 2 * (s + 1) * rank, here])
            pb[:, :, at] += part.reshape(nz, cols, chunk)
            return carry

        lax.fori_loop(0, rows // chunk, adapt, 0)

    got_cd, own_d = [], []

    def spread_d(p):
        arrive(got_ld[p])
        summed = nn(m2[...], line_d[p][...])
        col_d_out[p][...] = summed.astype(BF16)
        got_cd.append(
            exchange(col_d_out[p], col_d[p], rank, cd_s.at[p], cd_r.at[p], col_peer, ny)
        )
        own_d.append(summed[0:rank, :])

    rs_serve(0, 0)
    stores = [input_grad(0)]
    spread_d(0)
    rs_serve(0, 1)
    arrive(got_zu)
    total = u_out[z].astype(F32)
    for o in range(1, nz):
        total = total + u_in[o].astype(F32)
    for s, part in enumerate((total, swapped(total))):
        line_u[s * rank : (s + 1) * rank, :] = jnp.where(low_half, part, 0.0).astype(BF16)
    got_lu = exchange(line_u, line_u, 2 * rank, lu_s, lu_r, line_peer, nl, same=True)
    rs_serve(1, 0)
    for p in parts[1:]:
        spread_d(p)
    rs_serve(1, 1)
    stores.append(input_grad(1))
    rs_serve(2, 0)
    arrive(got_lu)
    summed_u = nn(m2[...], line_u[...])
    col_u_out[...] = summed_u.astype(BF16)
    got_cu = exchange(col_u_out, col_u, rank, cu_s, cu_r, col_peer, ny)
    own_u = summed_u[0:rank, :]
    for t in range(2, most):
        rs_serve(t, 0)
        rs_serve(t, 1)
    for h in range(QUARTERS):
        value = pb[z, h * part_rows : (h + 1) * part_rows, :]
        for direction in range(2):
            n = hops[direction][h]
            if n:
                value = value + rs_recv[direction, h, n - 1].astype(F32)
        values_ref[h * part_rows : (h + 1) * part_rows, :] = value.astype(BF16)

    for p in parts:
        arrive(got_cd[p])
        for o in range(1, ny):
            own_d[p] = own_d[p] + col_d[p][o * rank : (o + 1) * rank, :].astype(F32)
        down_ref[:, cuts[p][0] : cuts[p][0] + cuts[p][1]] = own_d[p]
    arrive(got_cu)
    for o in range(1, ny):
        own_u = own_u + col_u[o * rank : (o + 1) * rank, :].astype(F32)
    up_ref[...] = own_u[:, 0:cols]
    for copy in pending:
        copy.wait_send()
    for copy in stores:
        copy.wait()


def place_results(*refs):
    sem = refs[8]
    copies = [pltpu.make_async_copy(refs[i], refs[4 + i], sem.at[i]) for i in range(4)]
    for copy in copies:
        copy.start()
    for copy in copies:
        copy.wait()


def local(ny, nl, nz, hidden, weight, down, up, grad, index, table):
    tokens, width = hidden.shape
    rank = down.shape[2]
    cols = grad.shape[1]
    features = weight.shape[1]
    rows, part_rows = tokens // 2, cols // QUARTERS
    most = nz // 2
    vm = pltpu.VMEM
    dma = pltpu.SemaphoreType.DMA
    cuts = pieces(width)
    scratch = [
        pltpu.SMEM(index.shape, jnp.int32), pltpu.SMEM(table.shape, jnp.int32),
        vm((rank, cols), BF16), vm((width, features), BF16), vm((features, width), BF16),
        vm((width, tokens), BF16), vm((width, tokens), BF16), vm((2, nz, cols, 2 * rank), BF16),
        vm((nz, cols, tokens), BF16), vm((nz, cols, tokens), F32),
        vm((2, QUARTERS, most, part_rows, tokens), BF16), vm((2, QUARTERS, most, part_rows, tokens), BF16),
        vm((8 * nl, 128), jnp.int32),
        vm((nl * 2 * rank, ny * rank), BF16), vm((ny * rank, nl * 2 * rank), BF16),
        vm((ny * rank, 128), BF16), vm((nl * 2 * rank, 128), BF16), vm((nl * 2 * rank, 128), BF16),
        vm((nz, rank, 128), BF16), vm((nz, rank, 128), BF16), vm((nz, rank, 128), BF16),
        vm((nl * 2 * rank, 128), BF16), vm((ny * rank, 128), BF16), vm((ny * rank, 128), BF16),
        vm((4 * rank, rows), BF16), vm((2 * rank, rows), BF16), vm((width, 2 * rank), BF16),
        dma((6 + len(cuts),)), dma((2,)),
        *([dma((2, QUARTERS, most))] * 4),
    ]
    for n in (nl, ny, nl, nz, nz, nl, ny):
        scratch += [dma((n,)), dma((n,))]
    for n in (ny, 2 * nl, 2 * nl, 2, 2 * nl, ny, ny):
        scratch += [vm((n * rank, size), BF16) for _, size in cuts]
    for n in (ny, nl, nl, ny):
        scratch += [dma((len(cuts), n)), dma((len(cuts), n))]
    anywhere = pl.BlockSpec(memory_space=pl.ANY)
    inside = pl.BlockSpec(memory_space=pltpu.VMEM)
    values, hidden_grad, down_t, up_grad = pl.pallas_call(
        functools.partial(kernel, ny, nl, nz),
        out_shape=(
            vm((cols, tokens), BF16), vm((width, tokens), BF16), vm((rank, width), F32), vm((rank, cols), F32)
        ),
        in_specs=[pl.BlockSpec(memory_space=pltpu.HBM)] * 7,
        out_specs=(inside, anywhere, inside, inside),
        scratch_shapes=scratch,
        compiler_params=pltpu.CompilerParams(collective_id=0, has_side_effects=True, vmem_limit_bytes=58 << 20),
        name="adapter_step",
    )(index, table, grad.T, up[0], down[0].T, weight, hidden.T)
    results = (values, hidden_grad, down_t, up_grad)
    values, hidden_grad, down_t, up_grad = pl.pallas_call(
        place_results,
        out_shape=tuple(jax.ShapeDtypeStruct(r.shape, r.dtype) for r in results),
        in_specs=[anywhere] * 4,
        out_specs=(pl.BlockSpec(memory_space=pltpu.HBM),) * 4,
        scratch_shapes=[dma((4,))],
        compiler_params=pltpu.CompilerParams(vmem_limit_bytes=4 << 20),
        name="place_results",
    )(*results)
    return values.T, hidden_grad.T, down_t.T[None], up_grad[None]


def build(mesh, ny):
    nl, nz = mesh.shape["dp"] // ny, mesh.shape["mp"]
    return jax.shard_map(
        functools.partial(local, ny, nl, nz),
        mesh=mesh,
        in_specs=(
            P("dp", "mp"),
            P("mp", None),
            P("dp", "mp", None),
            P("dp", None, "mp"),
            P("dp", "mp"),
            P("dp"),
            P(),
        ),
        out_specs=(P("dp", "mp"), P("dp", "mp"), P("dp", "mp", None), P("dp", None, "mp")),
        check_vma=False,
    )


def solution(mesh):
    return build(mesh, NY)
```

```python
import functools

import jax
import jax.numpy as jnp
from jax import lax
from jax.experimental import pallas as pl
from jax.experimental.pallas import tpu as pltpu
from jax.sharding import PartitionSpec as P

F32 = jnp.float32
BF16 = jnp.bfloat16
MESH = pl.DeviceIdType.MESH
ORDER = (
    "base", "pass00", "masks", "pass01", "b1", "a0", "pass10", "a1",
    "pass11", "b2", "pass20", "masks2", "pass21", "low", "b3", "first",
    "gather", "down", "up", "second", "adapt", "turn", "ring00", "grad0",
    "down0", "ring01", "up1", "ring10", "down1", "ring11", "grad1", "ring20",
    "up2", "ring21", "ring30", "ring31",
)
QUARTERS = 4
NY = 8


def nt(a, b):
    return lax.dot_general(a, b, (((1,), (1,)), ((), ())), preferred_element_type=F32)


def nn(a, b):
    return jnp.dot(a, b, preferred_element_type=F32)


def iota(shape, dim):
    return lax.broadcasted_iota(jnp.int32, shape, dim)


def onehot(mask):
    return jnp.where(mask, 1.0, 0.0).astype(BF16)


def split(v):
    hi = v.astype(BF16)
    return hi, (v - hi.astype(F32)).astype(BF16)


def far_first(n):
    return sorted(range(1, n), key=lambda o: -min(o, n - o))


def pieces(width):
    first = (width // 2 + 127) // 128 * 128
    return [(at, size) for at, size in ((0, first), (first, width - first)) if size]


def kernel(
    ny, nl, nz,
    idx_hbm, tab_hbm, g_hbm, b_hbm, a_hbm, w_hbm, x_hbm,
    values_ref, hgrad_hbm, down_ref, up_ref,
    idx_ref, tab_ref, b_in, w, wt, x, hg, bt,
    gbuf, pb, rs_send, rs_recv,
    ids, m1, m2, col_b, line_b_out, line_b, z_b, u_out, u_in, line_u, col_u_out, col_u,
    low, back_t, a_rows,
    in_sem, out_sem, ag_s, ag_r, rs_s, rs_r,
    ids_s, ids_r, cb_s, cb_r, lb_s, lb_r, zb_s, zb_r, zu_s, zu_r, lu_s, lu_r, cu_s, cu_r,
    *by_piece,
):
    rank, cols = b_in.shape
    width, tokens = x.shape
    features = w.shape[1]
    rows = tokens // 2
    part_rows = cols // QUARTERS
    chunk = 256 if rows % 256 == 0 else rows
    cuts = pieces(width)
    parts = range(len(cuts))
    col_a, line_a_out, line_a, ab, line_d, col_d_out, col_d = (
        by_piece[i * len(cuts) : (i + 1) * len(cuts)] for i in range(7)
    )
    ca_s, ca_r, la_s, la_r, ld_s, ld_r, cd_s, cd_r = by_piece[7 * len(cuts) :]
    d, z = lax.axis_index("dp"), lax.axis_index("mp")
    c = lax.rem(d, 2)
    y = lax.rem(lax.div(d, 2), ny)
    xx = lax.div(d, 2 * ny)
    line = xx * 2 + c

    def line_peer(o):
        other = lax.rem(line + o, nl)
        return ((lax.div(other, 2) * ny + y) * 2 + lax.rem(other, 2), z)

    def col_peer(o):
        return ((xx * ny + lax.rem(y + o, ny)) * 2 + c, z)

    def z_peer(o):
        return (d, lax.rem(z + o, nz))

    barrier = pltpu.get_barrier_semaphore()
    peers = [z_peer(o) for o in range(1, nz)]
    peers += [col_peer(o) for o in range(1, ny)]
    peers += [line_peer(o) for o in range(1, nl)]
    for peer in peers:
        pl.semaphore_signal(barrier, inc=1, device_id=peer, device_id_type=MESH)

    loads = []
    wanted = [(idx_hbm, idx_ref), (tab_hbm, tab_ref), (g_hbm, gbuf.at[z]), (b_hbm, b_in)]
    wanted += [(a_hbm.at[:, pl.ds(*cuts[p])], col_a[p].at[pl.ds(0, rank), :]) for p in parts]
    wanted += [(w_hbm, w), (x_hbm, x)]
    for i, (src, dst) in enumerate(wanted):
        copy = pltpu.make_async_copy(src, dst, in_sem.at[i])
        copy.start()
        loads.append(copy)

    pending = []

    def send(src, dst, send_sem, recv_sem, peer):
        copy = pltpu.make_async_remote_copy(
            src_ref=src, dst_ref=dst, send_sem=send_sem, recv_sem=recv_sem,
            device_id=peer, device_id_type=MESH,
        )
        copy.start()
        pending.append(copy)
        return copy

    def block(ref, o, size):
        return ref.at[pl.ds(o * size, size), :]

    def exchange(out, into, size, send_sem, recv_sem, peer, n, same=False):
        return [
            send(
                block(out, 0 if same else o, size), block(into, o, size),
                send_sem.at[o], recv_sem.at[o], peer(o),
            )
            for o in far_first(n)
        ]

    def arrive(copies):
        for copy in copies:
            copy.wait_recv()

    loads[0].wait()
    loads[1].wait()
    s0, s1 = tab_ref[idx_ref[0]], tab_ref[idx_ref[1]]
    row, lane = iota((8, 128), 0), iota((8, 128), 1)
    second = jnp.where(row == 2, lax.shift_right_logical(lane, 5) & 1, row & 1)
    ids[0:8, :] = jnp.where(second == 1, s1, s0)

    low_half = iota((1, 128), 1) < cols

    def swapped(v):
        return pltpu.roll(v, cols, 1)

    loads[3].wait()
    wide = onehot(iota((cols, 128), 0) == iota((cols, 128), 1))
    col_b[0:rank, :] = nn(b_in[...], wide).astype(BF16)
    loads[2].wait()
    for p in parts:
        loads[4 + p].wait()
    pl.semaphore_wait(barrier, len(peers))

    most = nz // 2
    hops = [[most - ((h < QUARTERS // 2) == bool(side)) for h in range(QUARTERS)] for side in range(2)]

    def toward(direction, n):
        return lax.rem(z + (n if direction == 0 else nz - n), nz)

    def ring_peer(direction):
        return (d, toward(direction, 1))

    ag = {}

    def ag_send(direction, h, t):
        part = gbuf.at[toward(1 - direction, t) if t else z, pl.ds(h * part_rows, part_rows), :]
        ag[direction, h, t] = send(
            part, part, ag_s.at[direction, h, t], ag_r.at[direction, h, t], ring_peer(direction)
        )

    served = set()

    def ag_serve(t, *sides):
        for h in [h for h in range(QUARTERS) if h * 2 // QUARTERS in sides]:
            if ("ag", t, h) in served:
                continue
            served.add(("ag", t, h))
            for direction in range(2):
                n = hops[direction][h]
                if t < n:
                    ag[direction, h, t].wait_recv()
                    if t + 1 < n:
                        ag_send(direction, h, t + 1)

    for h in range(QUARTERS):
        for direction in range(2):
            if hops[direction][h]:
                ag_send(direction, h, 0)
    got_ids = exchange(ids, ids, 8, ids_s, ids_r, line_peer, nl, same=True)
    got_cb = exchange(col_b, col_b, rank, cb_s, cb_r, col_peer, ny, same=True)
    got_ca = [
        exchange(col_a[p], col_a[p], rank, ca_s.at[p], ca_r.at[p], col_peer, ny, same=True) for p in parts
    ]

    square = onehot(iota((features, features), 0) == iota((features, features), 1))
    tiles = features // 128
    got_lb, got_la, got_zb, up = [], [], [], []

    def base_blocks():
        loads[-2].wait()
        wt[...] = nt(square, w[...]).astype(BF16)
        loads[-1].wait()

        def base(step, carry):
            at = pl.ds(pl.multiple_of(step * chunk, chunk), chunk)
            part = nn(wt[...], x[:, at])
            for j in range(nz):
                pb[j, :, at] = part[j * cols : (j + 1) * cols, :]
            return carry

        lax.fori_loop(0, tokens // chunk, base, 0)

    def masks_in():
        arrive(got_ids)
        slot_in = (xx * ny + lax.rem(y + ny - lax.shift_right_logical(iota((rank, ny * rank), 1), 5), ny)) * 2 + c
        same_rank = (iota((rank, ny * rank), 1) & 31) == iota((rank, ny * rank), 0)
        for p in range(nl):
            q = (nl - p) % nl
            for s in range(2):
                own = ids[q * 8 + s : q * 8 + s + 1, :][:, 0:1]
                m1[(p * 2 + s) * rank : (p * 2 + s + 1) * rank, :] = onehot((slot_in == own) & same_rank)
    def gathered(out, into, size, n):
        total = out[0:size, :].astype(F32)
        for o in range(1, n):
            total = total + into[o * size : (o + 1) * size, :].astype(F32)
        return total

    def pick_a(p):
        arrive(got_ca[p])
        line_a_out[p][...] = nn(m1[...], col_a[p][...]).astype(BF16)
        got_la.append(exchange(line_a_out[p], line_a[p], 2 * rank, la_s.at[p], la_r.at[p], line_peer, nl))

    def pick_b():
        arrive(got_cb)
        line_b_out[...] = nn(m1[...], col_b[...]).astype(BF16)
        got_lb.extend(exchange(line_b_out, line_b, 2 * rank, lb_s, lb_r, line_peer, nl))

    def masks_out():
        per_tile = 128 // (2 * rank)
        across = []
        for i in range(nl // per_tile):
            q = i * per_tile
            across.append(jnp.where(low_half, ids[q * 8 + 2 : q * 8 + 3, :], ids[q * 8 + 10 : q * 8 + 11, :]))
        across = jnp.concatenate(across, axis=1)
        shape = (ny * rank, nl * 2 * rank)
        slot_out = (xx * ny + lax.rem(y + lax.shift_right_logical(iota((ny * rank, 1), 0), 5), ny)) * 2 + c
        m2[...] = onehot((slot_out == across) & ((iota(shape, 1) & 31) == (iota(shape, 0) & 31)))
    def share_b():
        arrive(got_lb)
        mine = gathered(line_b_out, line_b, 2 * rank, nl)
        z_b[z] = (mine[0:rank, :] + swapped(mine[rank:, :])).astype(BF16)
        got_zb[:] = [
            send(z_b.at[z], z_b.at[z], zb_s.at[o], zb_r.at[o], z_peer(o)) for o in far_first(nz)
        ]
    def low_rank():
        for p in parts:
            arrive(got_la[p])
            ab[p][...] = gathered(line_a_out[p], line_a[p], 2 * rank, nl).astype(BF16)
        for s in range(2):
            part = 0.0
            for p in parts:
                at, size = cuts[p]
                part = part + nn(ab[p][s * rank : (s + 1) * rank, :], x[at : at + size, s * rows : (s + 1) * rows])
            hi, rest = split(part)
            low[2 * s * rank : (2 * s + 1) * rank, :] = hi
            low[(2 * s + 1) * rank : (2 * s + 2) * rank, :] = rest

    def turn_a():
        for p in parts:
            at, size = cuts[p]
            turn = onehot(iota((size, size), 0) == iota((size, size), 1))
            a_rows[at : at + size, :] = nt(turn, ab[p][...]).astype(BF16)
    def whole_b():
        arrive(got_zb)
        blocks = [z_b[j].astype(F32) for j in range(nz)]
        both = [
            [jnp.where(low_half, blocks[2 * i], swapped(blocks[2 * i + 1])) for i in range(tiles)],
            [jnp.where(low_half, swapped(blocks[2 * i]), blocks[2 * i + 1]) for i in range(tiles)],
        ]
        up[:] = [jnp.concatenate(half, axis=1).astype(BF16) for half in both]
        for s in range(2):
            turned = nt(square, jnp.concatenate([up[s], up[s]], axis=0)).astype(BF16)
            bt[s] = turned.reshape(nz, cols, 2 * rank)

    def contribution(j, h):
        at = slice(h * part_rows, (h + 1) * part_rows)
        adapted = [
            nn(bt[s, j, at, :], low[2 * s * rank : 2 * (s + 1) * rank, :]) for s in range(2)
        ]
        return pb[j, at, :] + jnp.concatenate(adapted, axis=1)

    rs = {}

    def rs_go(direction, h, t):
        n = hops[direction][h]
        j = toward(direction, n - t)
        if t:
            value = pb[j, h * part_rows : (h + 1) * part_rows, :] + rs_recv[direction, h, t - 1].astype(F32)
        else:
            value = contribution(j, h)
        rs_send[direction, h, t] = value.astype(BF16)
        rs[direction, h, t] = send(
            rs_send.at[direction, h, t], rs_recv.at[direction, h, t],
            rs_s.at[direction, h, t], rs_r.at[direction, h, t], ring_peer(direction),
        )

    def rs_serve(t, *sides):
        for h in [h for h in range(QUARTERS) if h * 2 // QUARTERS in sides]:
            if ("rs", t, h) in served:
                continue
            served.add(("rs", t, h))
            for direction in range(2):
                n = hops[direction][h]
                if t < n:
                    rs[direction, h, t].wait_recv()
                    if t + 1 < n:
                        rs_go(direction, h, t + 1)

    def rs_begin(side):
        for h in [h for h in range(QUARTERS) if h * 2 // QUARTERS == side]:
            for direction in range(2):
                if hops[direction][h]:
                    rs_go(direction, h, 0)

    def grads(s, at=None):
        at = pl.ds(s * rows, rows) if at is None else at
        return gbuf[:, :, at].reshape(nz * cols, at.size)

    got_ld, got_zu, got_cd, own_d, stores, late = [], [], [], [], [], {}

    def gather_end():
        for t in range(most):
            ag_serve(t, 0, 1)

    def begin_d():
        for s in range(2):
            back_t[s * rank : (s + 1) * rank, :] = nn(up[s], grads(s)).astype(BF16)
        for p in parts:
            at, size = cuts[p]
            for s in range(2):
                line_d[p][s * rank : (s + 1) * rank, :] = nt(
                    back_t[s * rank : (s + 1) * rank, :], x[at : at + size, s * rows : (s + 1) * rows]
                ).astype(BF16)
            got_ld.append(
                exchange(line_d[p], line_d[p], 2 * rank, ld_s.at[p], ld_r.at[p], line_peer, nl, same=True)
            )

    def begin_u():
        ups = []
        for s in range(2):
            both = nt(low[2 * s * rank : 2 * (s + 1) * rank, :], grads(s))
            ups.append(both[0:rank, :] + both[rank:, :])
        for i in range(tiles):
            t0, t1 = (u[:, i * 128 : (i + 1) * 128] for u in ups)
            u_out[2 * i] = jnp.where(low_half, t0, swapped(t1)).astype(BF16)
            u_out[2 * i + 1] = jnp.where(low_half, swapped(t0), t1).astype(BF16)
        got_zu.extend(
            send(u_out.at[lax.rem(z + o, nz)], u_in.at[o], zu_s.at[o], zu_r.at[o], z_peer(o))
            for o in far_first(nz)
        )

    def input_grad(s):
        def body(step, carry):
            here = pl.ds(pl.multiple_of(step * chunk, chunk), chunk)
            at = pl.ds(pl.multiple_of(s * rows + step * chunk, chunk), chunk)
            hg[:, at] = (
                nn(w[...], grads(s, at))
                + nn(a_rows[:, s * rank : (s + 1) * rank], back_t[s * rank : (s + 1) * rank, here])
            ).astype(BF16)
            return carry

        lax.fori_loop(0, rows // chunk, body, 0)
        at = pl.ds(s * rows, rows)
        copy = pltpu.make_async_copy(hg.at[:, at], hgrad_hbm.at[:, at], out_sem.at[s])
        copy.start()
        stores.append(copy)

    def adapt_all():
        for s in range(2):
            turned = bt[s].reshape(nz * cols, 2 * rank)

            def adapt(step, carry):
                here = pl.ds(pl.multiple_of(step * chunk, chunk), chunk)
                at = pl.ds(pl.multiple_of(s * rows + step * chunk, chunk), chunk)
                part = nn(turned, low[2 * s * rank : 2 * (s + 1) * rank, here])
                pb[:, :, at] += part.reshape(nz, cols, chunk)
                return carry

            lax.fori_loop(0, rows // chunk, adapt, 0)

    def spread_d(p):
        arrive(got_ld[p])
        summed = nn(m2[...], line_d[p][...])
        col_d_out[p][...] = summed.astype(BF16)
        got_cd.append(
            exchange(col_d_out[p], col_d[p], rank, cd_s.at[p], cd_r.at[p], col_peer, ny)
        )
        own_d.append(summed[0:rank, :])

    def middle_u():
        arrive(got_zu)
        total = u_out[z].astype(F32)
        for o in range(1, nz):
            total = total + u_in[o].astype(F32)
        for s, part in enumerate((total, swapped(total))):
            line_u[s * rank : (s + 1) * rank, :] = jnp.where(low_half, part, 0.0).astype(BF16)
        late["line"] = exchange(line_u, line_u, 2 * rank, lu_s, lu_r, line_peer, nl, same=True)

    def spread_u():
        arrive(late["line"])
        summed = nn(m2[...], line_u[...])
        col_u_out[...] = summed.astype(BF16)
        late["column"] = exchange(col_u_out, col_u, rank, cu_s, cu_r, col_peer, ny)
        late["own"] = summed[0:rank, :]

    fronts = len(cuts) // 2
    steps = {
        "base": base_blocks, "masks": masks_in, "masks2": masks_out, "b1": pick_b, "b2": share_b, "b3": whole_b,
        "a0": lambda: pick_a(0), "a1": lambda: [pick_a(p) for p in parts[1:]], "low": low_rank, "turn": turn_a,
        "gather": gather_end, "first": lambda: rs_begin(0), "second": lambda: rs_begin(1),
        "down": begin_d, "up": begin_u, "adapt": adapt_all,
        "grad0": lambda: input_grad(0), "grad1": lambda: input_grad(1),
        "down0": lambda: [spread_d(p) for p in parts if p < max(fronts, 1)],
        "down1": lambda: [spread_d(p) for p in parts if p >= max(fronts, 1)],
        "up1": middle_u, "up2": spread_u,
    }
    for t in range(4):
        for side in range(2):
            steps[f"ring{t}{side}"] = functools.partial(rs_serve, t, side)
            steps[f"pass{t}{side}"] = functools.partial(ag_serve, t, side)
    for name in ORDER:
        if name[:4] not in ("ring", "pass") or int(name[4]) < most:
            steps[name]()

    for h in range(QUARTERS):
        value = pb[z, h * part_rows : (h + 1) * part_rows, :]
        for direction in range(2):
            n = hops[direction][h]
            if n:
                value = value + rs_recv[direction, h, n - 1].astype(F32)
        values_ref[h * part_rows : (h + 1) * part_rows, :] = value.astype(BF16)

    for p in parts:
        arrive(got_cd[p])
        for o in range(1, ny):
            own_d[p] = own_d[p] + col_d[p][o * rank : (o + 1) * rank, :].astype(F32)
        down_ref[:, cuts[p][0] : cuts[p][0] + cuts[p][1]] = own_d[p]
    arrive(late["column"])
    own_u = late["own"]
    for o in range(1, ny):
        own_u = own_u + col_u[o * rank : (o + 1) * rank, :].astype(F32)
    up_ref[...] = own_u[:, 0:cols]
    for copy in pending:
        copy.wait_send()
    for copy in stores:
        copy.wait()


def place_results(*refs):
    sem = refs[8]
    copies = [pltpu.make_async_copy(refs[i], refs[4 + i], sem.at[i]) for i in range(4)]
    for copy in copies:
        copy.start()
    for copy in copies:
        copy.wait()


def local(ny, nl, nz, hidden, weight, down, up, grad, index, table):
    tokens, width = hidden.shape
    rank = down.shape[2]
    cols = grad.shape[1]
    features = weight.shape[1]
    rows, part_rows = tokens // 2, cols // QUARTERS
    most = nz // 2
    vm = pltpu.VMEM
    dma = pltpu.SemaphoreType.DMA
    cuts = pieces(width)
    scratch = [
        pltpu.SMEM(index.shape, jnp.int32), pltpu.SMEM(table.shape, jnp.int32),
        vm((rank, cols), BF16), vm((width, features), BF16), vm((features, width), BF16),
        vm((width, tokens), BF16), vm((width, tokens), BF16), vm((2, nz, cols, 2 * rank), BF16),
        vm((nz, cols, tokens), BF16), vm((nz, cols, tokens), F32),
        vm((2, QUARTERS, most, part_rows, tokens), BF16), vm((2, QUARTERS, most, part_rows, tokens), BF16),
        vm((8 * nl, 128), jnp.int32),
        vm((nl * 2 * rank, ny * rank), BF16), vm((ny * rank, nl * 2 * rank), BF16),
        vm((ny * rank, 128), BF16), vm((nl * 2 * rank, 128), BF16), vm((nl * 2 * rank, 128), BF16),
        vm((nz, rank, 128), BF16), vm((nz, rank, 128), BF16), vm((nz, rank, 128), BF16),
        vm((nl * 2 * rank, 128), BF16), vm((ny * rank, 128), BF16), vm((ny * rank, 128), BF16),
        vm((4 * rank, rows), BF16), vm((2 * rank, rows), BF16), vm((width, 2 * rank), BF16),
        dma((6 + len(cuts),)), dma((2,)),
        *([dma((2, QUARTERS, most))] * 4),
    ]
    for n in (nl, ny, nl, nz, nz, nl, ny):
        scratch += [dma((n,)), dma((n,))]
    for n in (ny, 2 * nl, 2 * nl, 2, 2 * nl, ny, ny):
        scratch += [vm((n * rank, size), BF16) for _, size in cuts]
    for n in (ny, nl, nl, ny):
        scratch += [dma((len(cuts), n)), dma((len(cuts), n))]
    anywhere = pl.BlockSpec(memory_space=pl.ANY)
    inside = pl.BlockSpec(memory_space=pltpu.VMEM)
    values, hidden_grad, down_t, up_grad = pl.pallas_call(
        functools.partial(kernel, ny, nl, nz),
        out_shape=(
            vm((cols, tokens), BF16), vm((width, tokens), BF16), vm((rank, width), F32), vm((rank, cols), F32)
        ),
        in_specs=[pl.BlockSpec(memory_space=pltpu.HBM)] * 7,
        out_specs=(inside, anywhere, inside, inside),
        scratch_shapes=scratch,
        compiler_params=pltpu.CompilerParams(collective_id=0, has_side_effects=True, vmem_limit_bytes=58 << 20),
        name="adapter_step",
    )(index, table, grad.T, up[0], down[0].T, weight, hidden.T)
    results = (values, hidden_grad, down_t, up_grad)
    values, hidden_grad, down_t, up_grad = pl.pallas_call(
        place_results,
        out_shape=tuple(jax.ShapeDtypeStruct(r.shape, r.dtype) for r in results),
        in_specs=[anywhere] * 4,
        out_specs=(pl.BlockSpec(memory_space=pltpu.HBM),) * 4,
        scratch_shapes=[dma((4,))],
        compiler_params=pltpu.CompilerParams(vmem_limit_bytes=4 << 20),
        name="place_results",
    )(*results)
    return values.T, hidden_grad.T, down_t.T[None], up_grad[None]


def build(mesh, ny):
    nl, nz = mesh.shape["dp"] // ny, mesh.shape["mp"]
    return jax.shard_map(
        functools.partial(local, ny, nl, nz),
        mesh=mesh,
        in_specs=(
            P("dp", "mp"),
            P("mp", None),
            P("dp", "mp", None),
            P("dp", None, "mp"),
            P("dp", "mp"),
            P("dp"),
            P(),
        ),
        out_specs=(P("dp", "mp"), P("dp", "mp"), P("dp", "mp", None), P("dp", None, "mp")),
        check_vma=False,
    )


def solution(mesh):
    return build(mesh, NY)
```
